32 devices in a mesh: seq: 4 (over x, core), mp: 8 (over z, y).
Axes of the slice: x: 2, y: 2, z: 4, core: 2. Of those that a mesh axis runs over, the one named last changes fastest.
Arguments:
- queries: bfloat16 [1024, 4096], P('seq', 'mp'), may hold values from -15 to 15
- keys_values: bfloat16 [2, 1024, 4096], P(None, 'seq', 'mp'), may hold values from -6 to 6
- residual: bfloat16 [1024, 4096], P('seq', 'mp'), may hold values from -6 to 6
- cotangent: bfloat16 [1024, 4096], P('seq', 'mp'), may hold values from -6 to 6
- out_weight: bfloat16 [2, 4096, 4096], P(None, 'mp'), may hold values from -0.09375 to 0.09375
- kv_weight: bfloat16 [2, 4096, 4096], P(None, None, 'mp'), may hold values from -0.09375 to 0.09375
- bounds: int32 [2, 1024], replicated, may hold values from 0 to 767, as said below
- windows: int32 [64], P('mp'), may hold values from 1 to 127, as said below
Outputs:
- states_out: bfloat16 [1024, 4096], P('seq', 'mp')
- grad_states: bfloat16 [1024, 4096], P('seq', 'mp')
The draws below stay inside these ranges and needn't reach their ends.
Inputs may be any that keep to these rules, and one draw needn't show every extreme that they name: The encoder rows form 4 documents, each a run of consecutive positions; an encoder token's bounds are its own document's first and last position. The last document begins among the last 255 encoder positions. Decoder tokens belong to documents in reverse order, the first decoder token to the last document (other documents may have none), and carry that document's encoder bounds. `windows`: some head reaches exactly 127.
All inputs are finite; a program needn't handle non-finite values.
Results may differ from the reference program's by a relative error of at most 0.038.
Values may be sent and summed in bfloat16 or wider, within the bound.
A program may use at most 64 MiB of HBM per device.

```python
import jax
import jax.numpy as jnp
from jax import lax

D = 4096
HEADS = 64
HD = 64
ROWS = 256
WIN = 127
NDOC = 4
INNER = 4096
HL = 8
ENC_TOKENS = 768
DEC_TOKENS = 256
TOKENS = 1024
N_MP = 8


def draw_queries(key, part):
    base = jax.random.normal(jax.random.fold_in(key, 11), (TOKENS, HEADS * HD), jnp.float32)
    base = jnp.clip(base, -5.0, 5.0)
    return base.astype(jnp.bfloat16)


def draw_bounds(key, part):
    dec_count = TOKENS - ENC_TOKENS
    early_cuts = jax.random.permutation(jax.random.fold_in(key, 21), ENC_TOKENS - ROWS - 1)[:NDOC - 2] + 1
    last_cut = ENC_TOKENS - ROWS + 1 + jax.random.randint(jax.random.fold_in(key, 23), (1,), 0, ROWS - 1)
    enc_cuts = jnp.sort(jnp.concatenate([early_cuts.astype(jnp.int32), last_cut.astype(jnp.int32)])).astype(jnp.int32)
    starts = jnp.concatenate([jnp.zeros((1,), jnp.int32), enc_cuts])
    finals = jnp.concatenate([enc_cuts, jnp.full((1,), ENC_TOKENS, jnp.int32)]) - 1
    enc_pos = jnp.arange(ENC_TOKENS, dtype=jnp.int32)
    enc_doc = jnp.sum((enc_pos[:, None] >= enc_cuts[None, :]).astype(jnp.int32), axis=1)
    dec_cuts = jnp.sort(jax.random.randint(jax.random.fold_in(key, 22), (NDOC - 1,), 1, dec_count + 1)).astype(jnp.int32)
    dec_pos = jnp.arange(dec_count, dtype=jnp.int32)
    dec_doc = NDOC - 1 - jnp.sum((dec_pos[:, None] >= dec_cuts[None, :]).astype(jnp.int32), axis=1)
    doc_index = jnp.concatenate([enc_doc, dec_doc])
    return jnp.stack([starts[doc_index], finals[doc_index]]).astype(jnp.int32)


def draw_windows(key, part):
    widths = jax.random.randint(jax.random.fold_in(key, 31), (HEADS,), 1, WIN + 1)
    chosen = jax.random.randint(jax.random.fold_in(key, 32), (), 0, HEADS)
    return jnp.where(jnp.arange(HEADS) == chosen, WIN, widths).astype(jnp.int32)


def block_levels(stream_key, dims, split, low, top_value):
    gain, own = 1.0, jax.random.fold_in(stream_key, 6)
    for position, shards_of in split:
        draws = jnp.exp(jax.random.uniform(jax.random.fold_in(own, position), (shards_of,), jnp.float32, low / len(split), top_value / len(split)))
        gain = gain * jnp.repeat(draws, dims[position] // shards_of).reshape([-1 if axis == position else 1 for axis in range(len(dims))])
    return gain


def noise(key, dims, scale, most, cuts=(), held_as=jnp.bfloat16):
    drawn = scale * jax.random.normal(key, dims, jnp.float32)
    if cuts:
        drawn = drawn * block_levels(key, dims, cuts, -0.22, 0.18)
    return jnp.clip(drawn, -most, most).astype(held_as)


def setup_inputs(seed: int = 0) -> dict:
    arg_keys = jax.random.split(jax.random.key(seed), 9)
    queries = draw_queries(jax.random.fold_in(arg_keys[8], 71), 0)
    keys_values = noise(arg_keys[1], (2, TOKENS, INNER), 1.0, 6.0, ((1, 4), (2, 8)))
    residual = noise(arg_keys[2], (TOKENS, D), 1.0, 6.0, ((0, 4), (1, 8)))
    cotangent = noise(arg_keys[3], (TOKENS, D), 1.0, 6.0, ((0, 4), (1, 8)))
    out_weight = noise(arg_keys[4], (2, INNER, D), INNER ** -0.5, 0.09375, ((1, 8),))
    kv_weight = noise(arg_keys[5], (2, D, INNER), D ** -0.5, 0.09375, ((2, 8),))
    bounds = draw_bounds(jax.random.fold_in(arg_keys[8], 71), 0)
    windows = draw_windows(jax.random.fold_in(arg_keys[8], 71), 0)
    return {"queries": queries, "keys_values": keys_values, "residual": residual, "cotangent": cotangent, "out_weight": out_weight, "kv_weight": kv_weight, "bounds": bounds, "windows": windows}


def softmax_masked(scores, permitted):
    masked_scores = jnp.where(permitted, scores, -jnp.inf)
    row_top = jnp.max(masked_scores, axis=-1, keepdims=True)
    exp_scores = jnp.exp(masked_scores - row_top)
    return exp_scores / jnp.sum(exp_scores, axis=-1, keepdims=True)


def grouped_sum(left, right):
    def accumulate(running, pair):
        part_left, part_right = pair
        partial_term = jnp.dot(part_left, part_right, preferred_element_type=jnp.float32).astype(jnp.bfloat16)
        partial_term = lax.optimization_barrier(partial_term)
        return running + partial_term.astype(jnp.float32), None

    start_total = jnp.zeros((left.shape[1], right.shape[2]), jnp.float32)
    result_sum, unused_out = lax.scan(accumulate, start_total, (left, right))
    return result_sum


def block_total(parts):
    rounded = lax.optimization_barrier(parts.astype(jnp.bfloat16))
    return jnp.sum(rounded.astype(jnp.float32), axis=0).astype(jnp.bfloat16)


def by_head(array, count):
    return array.reshape(count, HEADS, HD).transpose(1, 0, 2)


def by_rows(array, count):
    return array.transpose(1, 0, 2).reshape(count, HEADS * HD)


def by_group(array, count):
    return array.reshape(count, N_MP, HL * HD).transpose(1, 0, 2)


def reference(queries, keys_values, residual, cotangent, out_weight, kv_weight, bounds, windows):
    score_scale = HD ** -0.5
    dec_blocks = DEC_TOKENS // ROWS
    first_pos = bounds[0]
    last_pos = bounds[1]
    enc_pos = jnp.arange(ENC_TOKENS, dtype=jnp.int32)
    doc_enc = (enc_pos[None, :] >= first_pos[:ENC_TOKENS, None]) & (enc_pos[None, :] <= last_pos[:ENC_TOKENS, None])
    distance = jnp.abs(enc_pos[:, None] - enc_pos[None, :])

    def local_head(inputs):
        head_query, head_key, head_value, reach_limit = inputs
        scores = jnp.dot(head_query, head_key.T, preferred_element_type=jnp.float32) * score_scale
        weights = softmax_masked(scores, doc_enc & (distance <= reach_limit))
        return jnp.dot(weights.astype(jnp.bfloat16), head_value, preferred_element_type=jnp.float32).astype(jnp.bfloat16)

    local_context = lax.map(local_head, (by_head(queries[:ENC_TOKENS], ENC_TOKENS), by_head(keys_values[0, :ENC_TOKENS], ENC_TOKENS), by_head(keys_values[1, :ENC_TOKENS], ENC_TOKENS), windows))
    local_context = by_rows(local_context, ENC_TOKENS)
    local_sum = grouped_sum(by_group(local_context, ENC_TOKENS), out_weight[0].reshape(N_MP, HL * HD, D))
    encoder_out = (residual[:ENC_TOKENS].astype(jnp.float32) + local_sum).astype(jnp.bfloat16)
    cross_keys = jnp.dot(encoder_out, kv_weight[0], preferred_element_type=jnp.float32).astype(jnp.bfloat16)
    cross_values = jnp.dot(encoder_out, kv_weight[1], preferred_element_type=jnp.float32).astype(jnp.bfloat16)

    doc_dec = (enc_pos[None, :] >= first_pos[ENC_TOKENS:, None]) & (enc_pos[None, :] <= last_pos[ENC_TOKENS:, None])
    context_grad = lax.dot_general(cotangent[ENC_TOKENS:], out_weight[1], (((1,), (1,)), ((), ())), preferred_element_type=jnp.float32).astype(jnp.bfloat16)

    def cross_head(inputs):
        head_query, head_key, head_value, head_grad = inputs
        scores = jnp.dot(head_query, head_key.T, preferred_element_type=jnp.float32) * score_scale
        weights = softmax_masked(scores, doc_dec)
        rounded = weights.astype(jnp.bfloat16)
        context = jnp.dot(rounded, head_value, preferred_element_type=jnp.float32).astype(jnp.bfloat16)
        row_dots = jnp.sum(head_grad.astype(jnp.float32) * context.astype(jnp.float32), axis=1)
        prob_grad = jnp.dot(head_grad, head_value.T, preferred_element_type=jnp.float32)
        score_grad = (weights * (prob_grad - row_dots[:, None])).astype(jnp.bfloat16)
        query_grad = (score_scale * jnp.dot(score_grad, head_key, preferred_element_type=jnp.float32)).astype(jnp.bfloat16)
        grad_blocks = score_grad.astype(jnp.float32).reshape(dec_blocks, ROWS, ENC_TOKENS)
        prob_blocks = rounded.astype(jnp.float32).reshape(dec_blocks, ROWS, ENC_TOKENS)
        query_blocks = head_query.astype(jnp.float32).reshape(dec_blocks, ROWS, HD)
        grad_rows = head_grad.astype(jnp.float32).reshape(dec_blocks, ROWS, HD)
        key_grad = block_total(score_scale * jnp.einsum("sqk,sqd->skd", grad_blocks, query_blocks))
        value_grad = block_total(jnp.einsum("sqk,sqd->skd", prob_blocks, grad_rows))
        return context, query_grad, key_grad, value_grad

    cross_context, query_grad, key_grad, value_grad = lax.map(cross_head, (by_head(queries[ENC_TOKENS:], DEC_TOKENS), by_head(cross_keys, ENC_TOKENS), by_head(cross_values, ENC_TOKENS), by_head(context_grad, DEC_TOKENS)))
    cross_context = by_rows(cross_context, DEC_TOKENS)
    query_grad = by_rows(query_grad, DEC_TOKENS)
    key_grad = by_rows(key_grad, ENC_TOKENS)
    value_grad = by_rows(value_grad, ENC_TOKENS)

    decoder_sum = grouped_sum(by_group(cross_context, DEC_TOKENS), out_weight[1].reshape(N_MP, HL * HD, D))
    decoder_out = (residual[ENC_TOKENS:].astype(jnp.float32) + decoder_sum).astype(jnp.bfloat16)
    grad_left = jnp.concatenate([by_group(key_grad, ENC_TOKENS), by_group(value_grad, ENC_TOKENS)], axis=2)
    weight_right = jnp.concatenate([kv_weight[0].reshape(D, N_MP, HL * HD).transpose(1, 2, 0), kv_weight[1].reshape(D, N_MP, HL * HD).transpose(1, 2, 0)], axis=1)
    encoder_grad = (cotangent[:ENC_TOKENS].astype(jnp.float32) + grouped_sum(grad_left, weight_right)).astype(jnp.bfloat16)
    return jnp.concatenate([encoder_out, decoder_out], axis=0), jnp.concatenate([encoder_grad, query_grad], axis=0)
```

```python
import functools

import jax
import jax.numpy as jnp
from jax import lax
from jax.experimental import pallas as pl
from jax.experimental.pallas import tpu as pltpu
from jax.sharding import PartitionSpec as P

HD = 64
WIN = 127


def with_halo(cells, sides, width):
    for axis, dim in sides:
        count = lax.axis_size(axis)
        ends = count - 1
        head = lax.slice_in_dim(cells, 0, width, axis=dim)
        tail = lax.slice_in_dim(cells, cells.shape[dim] - width, cells.shape[dim], axis=dim)
        cells = jnp.concatenate(
            [
                lax.ppermute(tail, axis, [(i, (i + 1) % count) for i in range(ends)]),
                cells,
                lax.ppermute(head, axis, [((i + 1) % count, i) for i in range(ends)]),
            ],
            axis=dim,
        )
    return cells


def softmax_masked(scores, permitted):
    masked_scores = jnp.where(permitted, scores, -jnp.inf)
    row_top = jnp.max(masked_scores, axis=-1, keepdims=True)
    exp_scores = jnp.exp(masked_scores - row_top)
    return exp_scores / jnp.sum(exp_scores, axis=-1, keepdims=True)


def shards(queries, keys_values, residual, cotangent, out_weight, kv_weight, bounds, windows):
    row_count = queries.shape[0]
    col_count = queries.shape[1]
    head_count = col_count // HD
    slab_count = lax.axis_size("seq")
    enc_slabs = 3 * slab_count // 4
    dec_slabs = slab_count - enc_slabs
    enc_tokens = enc_slabs * row_count
    token_count = slab_count * row_count
    dec_tokens = token_count - enc_tokens
    slab_index = lax.axis_index("seq")
    is_enc = slab_index < enc_slabs
    score_scale = HD ** (-0.5)
    own_pos = slab_index * row_count + jnp.arange(row_count, dtype=jnp.int32)
    own_first = lax.dynamic_slice_in_dim(bounds[0], slab_index * row_count, row_count)
    own_last = lax.dynamic_slice_in_dim(bounds[1], slab_index * row_count, row_count)
    query_heads = queries.reshape(row_count, head_count, HD)
    slice_cols = residual.shape[1]
    res_full, cot_full = (
        lax.all_gather(residual, "mp", axis=1, tiled=True),
        lax.all_gather(cotangent, "mp", axis=1, tiled=True),
    )
    model_width = cot_full.shape[1]
    rim_keys = with_halo(keys_values, (("seq", 1),), WIN)

    def local_part():
        span_count = rim_keys.shape[1]
        key_pos = slab_index * row_count - WIN + jnp.arange(span_count, dtype=jnp.int32)
        key_heads = rim_keys[0].reshape(span_count, head_count, HD)
        value_heads = rim_keys[1].reshape(span_count, head_count, HD)
        scores = (
            jnp.einsum("qhd,khd->hqk", query_heads, key_heads, preferred_element_type=jnp.float32)
            * score_scale
        )
        in_document = (key_pos[None, :] >= own_first[:, None]) & (
            key_pos[None, :] <= own_last[:, None]
        )
        distance = jnp.abs(own_pos[:, None] - key_pos[None, :])
        permitted = in_document[None] & (distance[None] <= windows[:, None, None])
        rounded = softmax_masked(scores, permitted).astype(jnp.bfloat16)
        context = jnp.einsum(
            "hqk,khd->qhd", rounded, value_heads, preferred_element_type=jnp.float32
        ).astype(jnp.bfloat16)
        return jnp.dot(
            context.reshape(row_count, col_count), out_weight[0], preferred_element_type=jnp.float32
        )

    head_partial = lax.cond(
        is_enc, local_part, lambda: jnp.zeros((row_count, model_width), jnp.float32)
    )
    attn_sum = lax.psum(head_partial.astype(jnp.bfloat16), "mp").astype(jnp.float32)
    hidden_full = (res_full.astype(jnp.float32) + attn_sum).astype(jnp.bfloat16)
    encoder_out = lax.dynamic_slice_in_dim(
        hidden_full, lax.axis_index("mp") * slice_cols, slice_cols, 1
    )

    def project_keys():
        key_proj = jnp.dot(hidden_full, kv_weight[0], preferred_element_type=jnp.float32).astype(
            jnp.bfloat16
        )
        value_proj = jnp.dot(hidden_full, kv_weight[1], preferred_element_type=jnp.float32).astype(
            jnp.bfloat16
        )
        return jnp.stack([key_proj, value_proj])

    cross_kv = lax.cond(
        is_enc, project_keys, lambda: jnp.zeros((2, row_count, col_count), jnp.bfloat16)
    )

    def context_gradient():
        return lax.dot_general(
            cot_full, out_weight[1], (((1,), (1,)), ((), ())), preferred_element_type=jnp.float32
        ).astype(jnp.bfloat16)

    dec_queries = lax.all_gather(queries, "seq", axis=0, tiled=True)[enc_tokens:]
    dec_heads = dec_queries.reshape(dec_tokens, head_count, HD)
    dec_first = bounds[0, enc_tokens:]
    dec_last = bounds[1, enc_tokens:]
    in_document = (own_pos[None, :] >= dec_first[:, None]) & (own_pos[None, :] <= dec_last[:, None])
    key_heads = cross_kv[0].reshape(row_count, head_count, HD)
    value_heads = cross_kv[1].reshape(row_count, head_count, HD)
    scores = (
        jnp.einsum("qhd,khd->hqk", dec_heads, key_heads, preferred_element_type=jnp.float32)
        * score_scale
    )
    masked_scores = jnp.where(in_document[None], scores, -jnp.inf)
    row_top = lax.pmax(jnp.max(masked_scores, axis=2), "seq")
    exp_scores = jnp.exp(masked_scores - row_top[:, :, None])
    row_total = lax.psum(jnp.sum(exp_scores, axis=2), "seq")
    weights = exp_scores / row_total[:, :, None]
    rounded = weights.astype(jnp.bfloat16)
    partial_ctx = jnp.einsum(
        "hqk,khd->qhd", rounded, value_heads, preferred_element_type=jnp.float32
    ).reshape(dec_tokens, col_count)
    context_all = lax.psum(partial_ctx.astype(jnp.bfloat16), "seq")
    dec_offset = jnp.maximum(slab_index - enc_slabs, 0) * row_count
    context = lax.dynamic_slice_in_dim(context_all, dec_offset, row_count, 0)
    out_part = lax.cond(
        is_enc,
        lambda: jnp.zeros((row_count, model_width), jnp.float32),
        lambda: jnp.dot(context, out_weight[1], preferred_element_type=jnp.float32),
    )
    grad_own = lax.cond(
        is_enc, lambda: jnp.zeros((row_count, col_count), jnp.bfloat16), context_gradient
    )
    grad_all = lax.all_gather(grad_own, "seq", axis=0, tiled=True)[enc_tokens:]
    grad_heads = grad_all.reshape(dec_tokens, head_count, HD)
    row_dots = jnp.einsum(
        "qhd,qhd->hq",
        grad_heads,
        context_all.reshape(dec_tokens, head_count, HD),
        preferred_element_type=jnp.float32,
    )
    prob_grad = jnp.einsum(
        "qhd,khd->hqk", grad_heads, value_heads, preferred_element_type=jnp.float32
    )
    score_grad = (weights * (prob_grad - row_dots[:, :, None])).astype(jnp.bfloat16)
    grad_blocks = score_grad.reshape(head_count, dec_slabs, row_count, row_count)
    prob_blocks = rounded.reshape(head_count, dec_slabs, row_count, row_count)
    query_blocks = dec_heads.reshape(dec_slabs, row_count, head_count, HD)
    grad_rows = grad_heads.reshape(dec_slabs, row_count, head_count, HD)
    key_parts = (
        score_scale
        * jnp.einsum(
            "hsqk,sqhd->skhd", grad_blocks, query_blocks, preferred_element_type=jnp.float32
        )
    ).astype(jnp.bfloat16)
    value_parts = jnp.einsum(
        "hsqk,sqhd->skhd", prob_blocks, grad_rows, preferred_element_type=jnp.float32
    ).astype(jnp.bfloat16)
    key_grad = (
        jnp.sum(key_parts.astype(jnp.float32), axis=0)
        .astype(jnp.bfloat16)
        .reshape(row_count, col_count)
    )
    value_grad = (
        jnp.sum(value_parts.astype(jnp.float32), axis=0)
        .astype(jnp.bfloat16)
        .reshape(row_count, col_count)
    )
    query_terms = score_scale * jnp.einsum(
        "hqk,khd->qhd", score_grad, key_heads, preferred_element_type=jnp.float32
    )
    query_sum = lax.psum(
        query_terms.reshape(dec_tokens, col_count).astype(jnp.bfloat16), "seq"
    ).astype(jnp.float32)
    query_grad = lax.dynamic_slice_in_dim(query_sum, dec_offset, row_count, 0).astype(jnp.bfloat16)
    contract = (((1,), (1,)), ((), ()))
    grad_terms = lax.dot_general(
        key_grad, kv_weight[0], contract, preferred_element_type=jnp.float32
    ) + lax.dot_general(value_grad, kv_weight[1], contract, preferred_element_type=jnp.float32)
    final_term = jnp.where(is_enc, grad_terms, out_part)
    final_share = lax.psum_scatter(
        final_term.astype(jnp.bfloat16), "mp", scatter_dimension=1, tiled=True
    ).astype(jnp.float32)
    base_rows = jnp.where(is_enc, cotangent, residual).astype(jnp.float32)
    final_rows = (base_rows + final_share).astype(jnp.bfloat16)
    states_out = jnp.where(is_enc, encoder_out, final_rows)
    grad_states = jnp.where(is_enc, final_rows, query_grad)
    return (states_out, grad_states)


F32 = jnp.float32
BF16 = jnp.bfloat16
LOW = -1e30
PAIR = 2 * HD
HALO = 128
NT = (((1,), (1,)), ((), ()))


def dot(a, b):
    return jnp.dot(a, b, preferred_element_type=F32)


def dot_nt(a, b):
    return lax.dot_general(a, b, NT, preferred_element_type=F32)


def layer_kernel(
    slabs,
    groups,
    q_ref,
    kv_ref,
    res_ref,
    cot_ref,
    ow_ref,
    kw_ref,
    bnd_ref,
    win_ref,
    states_ref,
    grads_ref,
    w_out,
    w_kv,
    kv_all,
    ctx,
    own_part,
    ysend,
    yrecv,
    zsend,
    zrecv,
    ysend2,
    yrecv2,
    zsend2,
    zrecv2,
    gath,
    acc,
    kv_new,
    dq,
    dg,
    e_buf,
    d_buf,
    stat,
    stat_in,
    fac,
    tbuf,
    ctx_in,
    qg_buf,
    qg_in,
    kvg,
    w_sem,
    kv_sem,
    halo_s,
    halo_r,
    ys_s,
    yr_s,
    zs_s,
    zr_s,
    ys2_s,
    yr2_s,
    zs2_s,
    zr2_s,
    gz_s,
    gz_r,
    gy_s,
    gy_r,
    dq_s,
    dq_r,
    dg_s,
    dg_r,
    st_s,
    st_r,
    cx_s,
    cx_r,
    qg_s,
    qg_r,
):
    rows, cols = q_ref.shape
    pairs = cols // PAIR
    heads = cols // HD
    enc = slabs - 1
    nz = groups // 2
    scale = HD ** (-0.5)
    s = lax.axis_index("seq")
    g = lax.axis_index("mp")
    z = g // 2
    y = lax.rem(g, 2)
    yo = 1 - y

    def remote(src, dst, send, recv, seq, mp):
        return pltpu.make_async_remote_copy(
            src_ref=src,
            dst_ref=dst,
            send_sem=send,
            recv_sem=recv,
            device_id={"seq": seq, "mp": mp},
            device_id_type=pl.DeviceIdType.MESH,
        )

    def arrived(dst, recv):
        pltpu.make_async_copy(dst, dst, recv).wait()

    is_enc = s < enc
    is_dec = s >= enc

    @pl.when(is_enc)
    def _():
        pltpu.make_async_copy(kv_ref, kv_all.at[:, pl.ds(HALO, rows)], kv_sem).start()
        pltpu.make_async_copy(ow_ref.at[0], w_out, w_sem.at[0]).start()
        pltpu.make_async_copy(kw_ref, w_kv, w_sem.at[1]).start()

    @pl.when(is_dec)
    def _():
        pltpu.make_async_copy(ow_ref.at[1], w_out, w_sem.at[0]).start()

    barrier = pltpu.get_barrier_semaphore()
    for k in range(1, slabs):
        pl.semaphore_signal(
            barrier,
            inc=1,
            device_id={"seq": lax.rem(s + k, slabs), "mp": g},
            device_id_type=pl.DeviceIdType.MESH,
        )
    for k in range(1, nz):
        pl.semaphore_signal(
            barrier,
            inc=1,
            device_id={"seq": s, "mp": lax.rem(z + k, nz) * 2 + y},
            device_id_type=pl.DeviceIdType.MESH,
        )
    pl.semaphore_signal(
        barrier,
        inc=1,
        device_id={"seq": s, "mp": z * 2 + yo},
        device_id_type=pl.DeviceIdType.MESH,
    )
    pl.semaphore_wait(barrier, slabs - 1 + nz - 1 + 1)

    lane = lax.broadcasted_iota(jnp.int32, (1, PAIR), 1)
    low_lane = lane < HD
    lane_masks = (
        jnp.where(low_lane, 1.0, 0.0).astype(BF16),
        jnp.where(low_lane, 0.0, 1.0).astype(BF16),
    )
    low_row = lax.broadcasted_iota(jnp.int32, (PAIR, 1), 0) < HD

    def pair_cols(p):
        return pl.ds(pl.multiple_of(p * PAIR, PAIR), PAIR)

    def chunk_cols(c):
        return pl.ds(pl.multiple_of(c * cols, cols), cols)

    def reduce_scatter(part, ysend, yrecv, zsend, zrecv, ys, yr, zs, zr):
        def first(k, carry):
            zt = lax.rem(z + 2 + k, nz)
            ysend[zt] = part(zt * 2 + yo)
            remote(ysend.at[zt], yrecv.at[zt], ys.at[zt], yr.at[zt], s, z * 2 + yo).start()
            return carry

        lax.fori_loop(0, nz, first, 0)

        def own(k, carry):
            zt = lax.rem(z + 2 + k, nz)
            own_part[zt] = part(zt * 2 + y)
            return carry

        lax.fori_loop(0, nz, own, 0)

        def second(k, carry):
            zt = lax.rem(z + 2 + k, nz)
            arrived(yrecv.at[zt], yr.at[zt])
            both = own_part[zt].astype(F32) + yrecv[zt].astype(F32)

            @pl.when(zt != z)
            def _():
                zsend[zt] = both.astype(BF16)
                remote(zsend.at[zt], zrecv.at[z], zs.at[zt], zr.at[z], s, zt * 2 + y).start()

            @pl.when(zt == z)
            def _():
                acc[0] = both

            return carry

        lax.fori_loop(0, nz, second, 0)

        def third(k, carry):
            zt = lax.rem(z + k, nz)
            arrived(zrecv.at[zt], zr.at[zt])
            acc[0] = acc[0] + zrecv[zt].astype(F32)
            return carry

        lax.fori_loop(1, nz, third, 0)
        return acc[0]

    def end_scatter(ysend, zsend, ys, zs):
        def last(k, carry):
            arrived(ysend.at[k], ys.at[k])
            return carry

        lax.fori_loop(0, nz, last, 0)

        def last_z(k, carry):
            zt = lax.rem(z + k, nz)
            arrived(zsend.at[zt], zs.at[zt])
            return carry

        lax.fori_loop(1, nz, last_z, 0)

    def gather(use):
        remote(gath.at[g], gath.at[g], gy_s.at[z], gy_r.at[z], s, z * 2 + yo).start()

        def spread(k, carry):
            zt = lax.rem(z + 1 + k, nz)
            remote(gath.at[g], gath.at[g], gz_s.at[zt], gz_r.at[z], s, zt * 2 + y).start()
            return carry

        lax.fori_loop(0, nz - 1, spread, 0)

        def begin(k, carry):
            zt = lax.rem(z + k, nz)
            c = zt * 2 + y

            @pl.when(k > 0)
            def _():
                arrived(gath.at[c], gz_r.at[zt])
                remote(gath.at[c], gath.at[c], gy_s.at[zt], gy_r.at[zt], s, z * 2 + yo).start()

            use(c)
            return carry

        lax.fori_loop(0, nz, begin, 0)

        def finish(k, carry):
            zt = lax.rem(z + k, nz)
            c = zt * 2 + yo
            arrived(gath.at[c], gy_r.at[zt])
            use(c)
            return carry

        lax.fori_loop(0, nz, finish, 0)

    def end_gather():
        def last(k, carry):
            arrived(gath.at[k * 2 + y], gy_s.at[k])
            return carry

        lax.fori_loop(0, nz, last, 0)

        def last_z(k, carry):
            zt = lax.rem(z + k, nz)
            arrived(gath.at[g], gz_s.at[zt])
            return carry

        lax.fori_loop(1, nz, last_z, 0)

    def joint_stats():
        top = stat_in[0, 0]
        for i in range(1, enc):
            top = jnp.maximum(top, stat_in[i, 0])
        total = jnp.zeros_like(top)
        dots = jnp.zeros_like(top)
        for i in range(enc):
            shift = jnp.exp(stat_in[i, 0] - top)
            total = total + shift * stat_in[i, 1]
            dots = dots + shift * stat_in[i, 2]
        return top, total, dots

    @pl.when(is_enc)
    def _():
        @pl.when(s + 1 < enc)
        def _():
            remote(
                kv_ref.at[:, pl.ds(rows - HALO, HALO)],
                kv_all.at[:, pl.ds(0, HALO)],
                halo_s.at[0],
                halo_r.at[0],
                s + 1,
                g,
            ).start()

        @pl.when(s > 0)
        def _():
            remote(
                kv_ref.at[:, pl.ds(0, HALO)],
                kv_all.at[:, pl.ds(HALO + rows, HALO)],
                halo_s.at[1],
                halo_r.at[1],
                s - 1,
                g,
            ).start()

        @pl.when(s == 0)
        def _():
            kv_all[:, pl.ds(0, HALO)] = jnp.zeros((2, HALO, cols), BF16)

        @pl.when(s == enc - 1)
        def _():
            kv_all[:, pl.ds(HALO + rows, HALO)] = jnp.zeros((2, HALO, cols), BF16)

        pltpu.make_async_copy(kv_ref, kv_all.at[:, pl.ds(HALO, rows)], kv_sem).wait()

        @pl.when(s > 0)
        def _():
            arrived(kv_all.at[:, pl.ds(0, HALO)], halo_r.at[0])

        @pl.when(s + 1 < enc)
        def _():
            arrived(kv_all.at[:, pl.ds(HALO + rows, HALO)], halo_r.at[1])

        span = rows + 2 * HALO
        key_pos = s * rows - HALO + lax.broadcasted_iota(jnp.int32, (span, 1), 0)
        own_pos = s * rows + lax.broadcasted_iota(jnp.int32, (1, rows), 1)
        far = jnp.abs(key_pos - own_pos)
        in_doc = (key_pos >= bnd_ref[0:1, :]) & (key_pos <= bnd_ref[1:2, :])
        far = jnp.where(in_doc, far, jnp.int32(1 << 20))

        def local_pair(p, carry):
            at = pair_cols(p)
            q_pair = q_ref[:, at]
            k_pair = kv_all[0, :, at]
            v_t = kv_all[1, :, at].T
            got = []
            for i in range(2):
                sc = dot_nt(k_pair, q_pair * lane_masks[i]) * scale
                sc = jnp.where(far <= win_ref[p * 2 + i], sc, LOW)
                e = jnp.exp(sc - jnp.max(sc, axis=0, keepdims=True))
                inv = 1.0 / jnp.sum(e, axis=0, keepdims=True)
                got.append(dot(v_t, (e * inv).astype(BF16)))
            ctx[:, at] = jnp.where(low_row, got[0], got[1]).T.astype(BF16)
            return carry

        lax.fori_loop(0, pairs, local_pair, 0)
        pltpu.make_async_copy(ow_ref.at[0], w_out, w_sem.at[0]).wait()
        total = reduce_scatter(
            lambda c: dot(ctx[...], w_out[:, chunk_cols(c)]).astype(BF16),
            ysend,
            yrecv,
            zsend,
            zrecv,
            ys_s,
            yr_s,
            zs_s,
            zr_s,
        )
        hidden = (res_ref[...].astype(F32) + total).astype(BF16)
        gath[g] = hidden
        states_ref[...] = hidden
        acc[...] = jnp.zeros_like(acc)
        pltpu.make_async_copy(kw_ref, w_kv, w_sem.at[1]).wait()

        def project(c):
            block = gath[c]
            acc[0] = acc[0] + dot(block, w_kv[0, chunk_cols(c), :])
            acc[1] = acc[1] + dot(block, w_kv[1, chunk_cols(c), :])

        gather(project)
        kv_new[...] = acc[...].astype(BF16)
        arrived(dq, dq_r)
        arrived(dg, dg_r)

        tok_pos = s * rows + lax.broadcasted_iota(jnp.int32, (rows, 1), 0)
        seen = (tok_pos >= bnd_ref[2:3, :]) & (tok_pos <= bnd_ref[3:4, :])

        def cross_pair(p, carry):
            at = pair_cols(p)
            q_pair = dq[:, at]
            g_pair = dg[:, at]
            k_pair = kv_new[0, :, at]
            v_pair = kv_new[1, :, at]
            v_t = v_pair.T
            got = []
            for i in range(2):
                sc = dot_nt(k_pair, q_pair * lane_masks[i]) * scale
                sc = jnp.where(seen, sc, LOW)
                top = jnp.max(sc, axis=0, keepdims=True)
                e = jnp.exp(sc - top)
                dp = dot_nt(v_pair, g_pair * lane_masks[i])
                h = p * 2 + i
                e_buf[h] = e
                d_buf[h] = dp
                stat[0, pl.ds(h, 1), :] = top
                stat[1, pl.ds(h, 1), :] = jnp.sum(e, axis=0, keepdims=True)
                stat[2, pl.ds(h, 1), :] = jnp.sum(e * dp, axis=0, keepdims=True)
                got.append(dot(v_t, e.astype(BF16)))
            tbuf[pair_cols(p), :] = jnp.where(low_row, got[0], got[1]).astype(BF16)
            return carry

        lax.fori_loop(0, pairs, cross_pair, 0)
        for k in range(1, slabs):
            to = lax.rem(s + k, slabs)
            remote(stat, stat_in.at[s], st_s.at[k - 1], st_r.at[s], to, g).start()
        remote(tbuf, ctx_in.at[s], cx_s, cx_r.at[s], enc, g).start()
        stat_in[s] = stat[...]
        for k in range(1, enc):
            at = lax.rem(s + k, enc)
            arrived(stat_in.at[at], st_r.at[at])
        top, total, dots = joint_stats()
        fac[0] = jnp.exp(stat[0] - top) / total
        fac[1] = dots / total

        def grad_pair(p, carry):
            at = pair_cols(p)
            q_pair = dq[:, at]
            g_pair = dg[:, at]
            k_t = kv_new[0, :, at].T
            kg, vg, qg = [], [], []
            for i in range(2):
                h = p * 2 + i
                w = e_buf[h] * fac[0, pl.ds(h, 1), :]
                ds = (w * (d_buf[h] - fac[1, pl.ds(h, 1), :])).astype(BF16)
                vg.append(dot(w.astype(BF16), g_pair))
                kg.append(dot(ds, q_pair))
                qg.append(dot(k_t, ds))
            kvg[0, :, at] = (scale * jnp.where(low_lane, kg[0], kg[1])).astype(BF16)
            kvg[1, :, at] = jnp.where(low_lane, vg[0], vg[1]).astype(BF16)
            qg_buf[pair_cols(p), :] = (scale * jnp.where(low_row, qg[0], qg[1])).astype(BF16)
            return carry

        lax.fori_loop(0, pairs, grad_pair, 0)
        remote(qg_buf, qg_in.at[s], qg_s, qg_r.at[s], enc, g).start()
        total = reduce_scatter(
            lambda c: (
                dot_nt(kvg[0], w_kv[0, chunk_cols(c), :]) + dot_nt(kvg[1], w_kv[1, chunk_cols(c), :])
            ).astype(BF16),
            ysend2,
            yrecv2,
            zsend2,
            zrecv2,
            ys2_s,
            yr2_s,
            zs2_s,
            zr2_s,
        )
        grads_ref[...] = (cot_ref[...].astype(F32) + total).astype(BF16)

        @pl.when(s + 1 < enc)
        def _():
            arrived(kv_ref.at[:, pl.ds(rows - HALO, HALO)], halo_s.at[0])

        @pl.when(s > 0)
        def _():
            arrived(kv_ref.at[:, pl.ds(0, HALO)], halo_s.at[1])

        end_scatter(ysend, zsend, ys_s, zs_s)
        end_gather()
        for k in range(1, slabs):
            arrived(stat, st_s.at[k - 1])
        arrived(tbuf, cx_s)
        arrived(qg_buf, qg_s)
        end_scatter(ysend2, zsend2, ys2_s, zs2_s)

    @pl.when(is_dec)
    def _():
        for k in range(enc):
            remote(q_ref, dq, dq_s.at[k], dq_r, k, g).start()
        gath[g] = cot_ref[...]
        acc[0] = jnp.zeros((rows, cols), F32)
        pltpu.make_async_copy(ow_ref.at[1], w_out, w_sem.at[0]).wait()

        def back(c):
            acc[0] = acc[0] + dot_nt(gath[c], w_out[:, chunk_cols(c)])

        gather(back)
        dg[...] = acc[0].astype(BF16)
        for k in range(enc):
            remote(dg, dg, dg_s.at[k], dg_r, k, g).start()
        for k in range(enc):
            arrived(stat_in.at[k], st_r.at[k])
        top, total, dots = joint_stats()
        shares = [jnp.exp(stat_in[k, 0] - top) / total for k in range(enc)]
        for k in range(enc):
            arrived(ctx_in.at[k], cx_r.at[k])
        for h in range(heads):
            at = slice(h * HD, (h + 1) * HD)
            part = jnp.zeros((HD, rows), F32)
            for k in range(enc):
                part = part + shares[k][h : h + 1, :] * ctx_in[k, at, :].astype(F32)
            d_buf[h, 0:HD, :] = part
        for p in range(pairs):
            both = jnp.concatenate([d_buf[2 * p, 0:HD, :], d_buf[2 * p + 1, 0:HD, :]], axis=0)
            ctx[:, p * PAIR : (p + 1) * PAIR] = both.T.astype(BF16)
        total = reduce_scatter(
            lambda c: dot(ctx[...], w_out[:, chunk_cols(c)]).astype(BF16),
            ysend2,
            yrecv2,
            zsend2,
            zrecv2,
            ys2_s,
            yr2_s,
            zs2_s,
            zr2_s,
        )
        states_ref[...] = (res_ref[...].astype(F32) + total).astype(BF16)
        for k in range(enc):
            arrived(qg_in.at[k], qg_r.at[k])
        for p in range(pairs):
            at = slice(p * PAIR, (p + 1) * PAIR)
            part = jnp.zeros((PAIR, rows), F32)
            for k in range(enc):
                part = part + qg_in[k, at, :].astype(F32)
            grads_ref[:, at] = part.T.astype(BF16)
        for k in range(enc):
            arrived(q_ref, dq_s.at[k])
            arrived(dg, dg_s.at[k])
        end_gather()
        end_scatter(ysend2, zsend2, ys2_s, zs2_s)


def layer(slabs, groups, queries, keys_values, residual, cotangent, out_weight, kv_weight, bounds, windows):
    rows, cols = queries.shape
    heads = cols // HD
    nz = groups // 2
    enc = slabs - 1
    width = out_weight.shape[2]
    own = lax.dynamic_slice_in_dim(bounds, lax.axis_index("seq") * rows, rows, 1)
    bnd = jnp.concatenate([own, bounds[:, enc * rows :]], axis=0)
    dma = pltpu.SemaphoreType.DMA
    blocks = lambda n: pltpu.VMEM((n, rows, cols), BF16)
    vmem = pl.BlockSpec(memory_space=pltpu.VMEM)
    hbm = pl.BlockSpec(memory_space=pl.ANY)
    return pl.pallas_call(
        functools.partial(layer_kernel, slabs, groups),
        out_shape=(jax.ShapeDtypeStruct((rows, cols), BF16),) * 2,
        in_specs=[vmem] * 4 + [hbm] * 2 + [vmem, pl.BlockSpec(memory_space=pltpu.SMEM)],
        out_specs=(vmem, vmem),
        scratch_shapes=[
            pltpu.VMEM((cols, width), BF16),
            pltpu.VMEM((2, width, cols), BF16),
            pltpu.VMEM((2, rows + 2 * HALO, cols), BF16),
            pltpu.VMEM((rows, cols), BF16),
            blocks(nz),
            blocks(nz),
            blocks(nz),
            blocks(nz),
            blocks(nz),
            blocks(nz),
            blocks(nz),
            blocks(nz),
            blocks(nz),
            blocks(groups),
            pltpu.VMEM((2, rows, cols), F32),
            blocks(2),
            pltpu.VMEM((rows, cols), BF16),
            pltpu.VMEM((rows, cols), BF16),
            pltpu.VMEM((heads, rows, rows), F32),
            pltpu.VMEM((heads, rows, rows), F32),
            pltpu.VMEM((3, heads, rows), F32),
            pltpu.VMEM((slabs, 3, heads, rows), F32),
            pltpu.VMEM((2, heads, rows), F32),
            pltpu.VMEM((cols, rows), BF16),
            pltpu.VMEM((enc, cols, rows), BF16),
            pltpu.VMEM((cols, rows), BF16),
            pltpu.VMEM((enc, cols, rows), BF16),
            blocks(2),
            dma((2,)),
            dma,
            dma((2,)),
            dma((2,)),
        ]
        + [dma((nz,))] * 12
        + [
            dma((enc,)),
            dma,
            dma((enc,)),
            dma,
            dma((enc,)),
            dma((slabs,)),
            dma,
            dma((enc,)),
            dma,
            dma((enc,)),
        ],
        compiler_params=pltpu.CompilerParams(
            collective_id=0, has_side_effects=True, vmem_limit_bytes=60 * 1024 * 1024
        ),
    )(queries, keys_values, residual, cotangent, out_weight, kv_weight, bnd, windows)


def one_decoder_slab(mesh):
    slabs, groups = mesh.shape["seq"], mesh.shape["mp"]
    return slabs - 3 * slabs // 4 == 1 and groups % 2 == 0


def solution(mesh):
    body = shards
    if one_decoder_slab(mesh):
        body = functools.partial(layer, mesh.shape["seq"], mesh.shape["mp"])

    return jax.shard_map(
        body,
        mesh=mesh,
        in_specs=(
            P("seq", "mp"),
            P(None, "seq", "mp"),
            P("seq", "mp"),
            P("seq", "mp"),
            P(None, "mp", None),
            P(None, None, "mp"),
            P(),
            P("mp"),
        ),
        out_specs=(P("seq", "mp"), P("seq", "mp")),
        check_vma=False,
    )
```

```python
import functools

import jax
import jax.numpy as jnp
from jax import lax
from jax.experimental import pallas as pl
from jax.experimental.pallas import tpu as pltpu
from jax.sharding import PartitionSpec as P

HD = 64
WIN = 127


def with_halo(cells, sides, width):
    for axis, dim in sides:
        count = lax.axis_size(axis)
        ends = count - 1
        head = lax.slice_in_dim(cells, 0, width, axis=dim)
        tail = lax.slice_in_dim(cells, cells.shape[dim] - width, cells.shape[dim], axis=dim)
        cells = jnp.concatenate(
            [
                lax.ppermute(tail, axis, [(i, (i + 1) % count) for i in range(ends)]),
                cells,
                lax.ppermute(head, axis, [((i + 1) % count, i) for i in range(ends)]),
            ],
            axis=dim,
        )
    return cells


def softmax_masked(scores, permitted):
    masked_scores = jnp.where(permitted, scores, -jnp.inf)
    row_top = jnp.max(masked_scores, axis=-1, keepdims=True)
    exp_scores = jnp.exp(masked_scores - row_top)
    return exp_scores / jnp.sum(exp_scores, axis=-1, keepdims=True)


def shards(queries, keys_values, residual, cotangent, out_weight, kv_weight, bounds, windows):
    row_count = queries.shape[0]
    col_count = queries.shape[1]
    head_count = col_count // HD
    slab_count = lax.axis_size("seq")
    enc_slabs = 3 * slab_count // 4
    dec_slabs = slab_count - enc_slabs
    enc_tokens = enc_slabs * row_count
    token_count = slab_count * row_count
    dec_tokens = token_count - enc_tokens
    slab_index = lax.axis_index("seq")
    is_enc = slab_index < enc_slabs
    score_scale = HD ** (-0.5)
    own_pos = slab_index * row_count + jnp.arange(row_count, dtype=jnp.int32)
    own_first = lax.dynamic_slice_in_dim(bounds[0], slab_index * row_count, row_count)
    own_last = lax.dynamic_slice_in_dim(bounds[1], slab_index * row_count, row_count)
    query_heads = queries.reshape(row_count, head_count, HD)
    slice_cols = residual.shape[1]
    res_full, cot_full = (
        lax.all_gather(residual, "mp", axis=1, tiled=True),
        lax.all_gather(cotangent, "mp", axis=1, tiled=True),
    )
    model_width = cot_full.shape[1]
    rim_keys = with_halo(keys_values, (("seq", 1),), WIN)

    def local_part():
        span_count = rim_keys.shape[1]
        key_pos = slab_index * row_count - WIN + jnp.arange(span_count, dtype=jnp.int32)
        key_heads = rim_keys[0].reshape(span_count, head_count, HD)
        value_heads = rim_keys[1].reshape(span_count, head_count, HD)
        scores = (
            jnp.einsum("qhd,khd->hqk", query_heads, key_heads, preferred_element_type=jnp.float32)
            * score_scale
        )
        in_document = (key_pos[None, :] >= own_first[:, None]) & (
            key_pos[None, :] <= own_last[:, None]
        )
        distance = jnp.abs(own_pos[:, None] - key_pos[None, :])
        permitted = in_document[None] & (distance[None] <= windows[:, None, None])
        rounded = softmax_masked(scores, permitted).astype(jnp.bfloat16)
        context = jnp.einsum(
            "hqk,khd->qhd", rounded, value_heads, preferred_element_type=jnp.float32
        ).astype(jnp.bfloat16)
        return jnp.dot(
            context.reshape(row_count, col_count), out_weight[0], preferred_element_type=jnp.float32
        )

    head_partial = lax.cond(
        is_enc, local_part, lambda: jnp.zeros((row_count, model_width), jnp.float32)
    )
    attn_sum = lax.psum(head_partial.astype(jnp.bfloat16), "mp").astype(jnp.float32)
    hidden_full = (res_full.astype(jnp.float32) + attn_sum).astype(jnp.bfloat16)
    encoder_out = lax.dynamic_slice_in_dim(
        hidden_full, lax.axis_index("mp") * slice_cols, slice_cols, 1
    )

    def project_keys():
        key_proj = jnp.dot(hidden_full, kv_weight[0], preferred_element_type=jnp.float32).astype(
            jnp.bfloat16
        )
        value_proj = jnp.dot(hidden_full, kv_weight[1], preferred_element_type=jnp.float32).astype(
            jnp.bfloat16
        )
        return jnp.stack([key_proj, value_proj])

    cross_kv = lax.cond(
        is_enc, project_keys, lambda: jnp.zeros((2, row_count, col_count), jnp.bfloat16)
    )

    def context_gradient():
        return lax.dot_general(
            cot_full, out_weight[1], (((1,), (1,)), ((), ())), preferred_element_type=jnp.float32
        ).astype(jnp.bfloat16)

    dec_queries = lax.all_gather(queries, "seq", axis=0, tiled=True)[enc_tokens:]
    dec_heads = dec_queries.reshape(dec_tokens, head_count, HD)
    dec_first = bounds[0, enc_tokens:]
    dec_last = bounds[1, enc_tokens:]
    in_document = (own_pos[None, :] >= dec_first[:, None]) & (own_pos[None, :] <= dec_last[:, None])
    key_heads = cross_kv[0].reshape(row_count, head_count, HD)
    value_heads = cross_kv[1].reshape(row_count, head_count, HD)
    scores = (
        jnp.einsum("qhd,khd->hqk", dec_heads, key_heads, preferred_element_type=jnp.float32)
        * score_scale
    )
    masked_scores = jnp.where(in_document[None], scores, -jnp.inf)
    row_top = lax.pmax(jnp.max(masked_scores, axis=2), "seq")
    exp_scores = jnp.exp(masked_scores - row_top[:, :, None])
    row_total = lax.psum(jnp.sum(exp_scores, axis=2), "seq")
    weights = exp_scores / row_total[:, :, None]
    rounded = weights.astype(jnp.bfloat16)
    partial_ctx = jnp.einsum(
        "hqk,khd->qhd", rounded, value_heads, preferred_element_type=jnp.float32
    ).reshape(dec_tokens, col_count)
    context_all = lax.psum(partial_ctx.astype(jnp.bfloat16), "seq")
    dec_offset = jnp.maximum(slab_index - enc_slabs, 0) * row_count
    context = lax.dynamic_slice_in_dim(context_all, dec_offset, row_count, 0)
    out_part = lax.cond(
        is_enc,
        lambda: jnp.zeros((row_count, model_width), jnp.float32),
        lambda: jnp.dot(context, out_weight[1], preferred_element_type=jnp.float32),
    )
    grad_own = lax.cond(
        is_enc, lambda: jnp.zeros((row_count, col_count), jnp.bfloat16), context_gradient
    )
    grad_all = lax.all_gather(grad_own, "seq", axis=0, tiled=True)[enc_tokens:]
    grad_heads = grad_all.reshape(dec_tokens, head_count, HD)
    row_dots = jnp.einsum(
        "qhd,qhd->hq",
        grad_heads,
        context_all.reshape(dec_tokens, head_count, HD),
        preferred_element_type=jnp.float32,
    )
    prob_grad = jnp.einsum(
        "qhd,khd->hqk", grad_heads, value_heads, preferred_element_type=jnp.float32
    )
    score_grad = (weights * (prob_grad - row_dots[:, :, None])).astype(jnp.bfloat16)
    grad_blocks = score_grad.reshape(head_count, dec_slabs, row_count, row_count)
    prob_blocks = rounded.reshape(head_count, dec_slabs, row_count, row_count)
    query_blocks = dec_heads.reshape(dec_slabs, row_count, head_count, HD)
    grad_rows = grad_heads.reshape(dec_slabs, row_count, head_count, HD)
    key_parts = (
        score_scale
        * jnp.einsum(
            "hsqk,sqhd->skhd", grad_blocks, query_blocks, preferred_element_type=jnp.float32
        )
    ).astype(jnp.bfloat16)
    value_parts = jnp.einsum(
        "hsqk,sqhd->skhd", prob_blocks, grad_rows, preferred_element_type=jnp.float32
    ).astype(jnp.bfloat16)
    key_grad = (
        jnp.sum(key_parts.astype(jnp.float32), axis=0)
        .astype(jnp.bfloat16)
        .reshape(row_count, col_count)
    )
    value_grad = (
        jnp.sum(value_parts.astype(jnp.float32), axis=0)
        .astype(jnp.bfloat16)
        .reshape(row_count, col_count)
    )
    query_terms = score_scale * jnp.einsum(
        "hqk,khd->qhd", score_grad, key_heads, preferred_element_type=jnp.float32
    )
    query_sum = lax.psum(
        query_terms.reshape(dec_tokens, col_count).astype(jnp.bfloat16), "seq"
    ).astype(jnp.float32)
    query_grad = lax.dynamic_slice_in_dim(query_sum, dec_offset, row_count, 0).astype(jnp.bfloat16)
    contract = (((1,), (1,)), ((), ()))
    grad_terms = lax.dot_general(
        key_grad, kv_weight[0], contract, preferred_element_type=jnp.float32
    ) + lax.dot_general(value_grad, kv_weight[1], contract, preferred_element_type=jnp.float32)
    final_term = jnp.where(is_enc, grad_terms, out_part)
    final_share = lax.psum_scatter(
        final_term.astype(jnp.bfloat16), "mp", scatter_dimension=1, tiled=True
    ).astype(jnp.float32)
    base_rows = jnp.where(is_enc, cotangent, residual).astype(jnp.float32)
    final_rows = (base_rows + final_share).astype(jnp.bfloat16)
    states_out = jnp.where(is_enc, encoder_out, final_rows)
    grad_states = jnp.where(is_enc, final_rows, query_grad)
    return (states_out, grad_states)


F32 = jnp.float32
BF16 = jnp.bfloat16
LOW = -1e30
PAIR = 2 * HD
HALO = 128
BLOCKS = 2
NT = (((1,), (1,)), ((), ()))


def dot(a, b):
    return jnp.dot(a, b, preferred_element_type=F32)


def dot_nt(a, b):
    return lax.dot_general(a, b, NT, preferred_element_type=F32)


def layer_kernel(
    slabs,
    groups,
    q_ref,
    kv_ref,
    res_ref,
    cot_ref,
    ow_ref,
    kw_ref,
    bnd_ref,
    win_ref,
    states_ref,
    grads_ref,
    w_out,
    w_kv,
    kv_all,
    ctx,
    own_part,
    ysend,
    yrecv,
    zsend,
    zrecv,
    ysend2,
    yrecv2,
    zsend2,
    zrecv2,
    gath,
    acc,
    tot,
    kv_new,
    dq,
    dg,
    e_buf,
    d_buf,
    stat,
    stat_in,
    fac,
    tbuf,
    ctx_in,
    qg_buf,
    qg_in,
    kvg,
    w_sem,
    kv_sem,
    halo_s,
    halo_r,
    ys_s,
    yr_s,
    zs_s,
    zr_s,
    ys2_s,
    yr2_s,
    zs2_s,
    zr2_s,
    gu_s,
    gd_s,
    gz_r,
    gy_s,
    gy_r,
    dq_s,
    dq_r,
    dg_s,
    dg_r,
    st_s,
    st_r,
    cx_s,
    cx_r,
    qg_s,
    qg_r,
):
    rows, cols = q_ref.shape
    pairs = cols // PAIR
    heads = cols // HD
    enc = slabs - 1
    sub = rows // BLOCKS
    nz = groups // 2
    scale = HD ** (-0.5)
    s = lax.axis_index("seq")
    g = lax.axis_index("mp")
    z = g // 2
    y = lax.rem(g, 2)
    yo = 1 - y

    def remote(src, dst, send, recv, seq, mp):
        return pltpu.make_async_remote_copy(
            src_ref=src,
            dst_ref=dst,
            send_sem=send,
            recv_sem=recv,
            device_id={"seq": seq, "mp": mp},
            device_id_type=pl.DeviceIdType.MESH,
        )

    def arrived(dst, recv):
        pltpu.make_async_copy(dst, dst, recv).wait()

    is_enc = s < enc
    is_dec = s >= enc

    @pl.when(is_enc)
    def _():
        pltpu.make_async_copy(kv_ref, kv_all.at[:, pl.ds(HALO, rows)], kv_sem).start()
        pltpu.make_async_copy(ow_ref.at[0], w_out, w_sem.at[0]).start()
        pltpu.make_async_copy(kw_ref, w_kv, w_sem.at[1]).start()

    @pl.when(is_dec)
    def _():
        pltpu.make_async_copy(ow_ref.at[1], w_out, w_sem.at[0]).start()

    barrier = pltpu.get_barrier_semaphore()
    for k in range(1, slabs):
        pl.semaphore_signal(
            barrier,
            inc=1,
            device_id={"seq": lax.rem(s + k, slabs), "mp": g},
            device_id_type=pl.DeviceIdType.MESH,
        )

    @pl.when(z > 0)
    def _():
        pl.semaphore_signal(
            barrier,
            inc=1,
            device_id={"seq": s, "mp": (z - 1) * 2 + y},
            device_id_type=pl.DeviceIdType.MESH,
        )

    @pl.when(z < nz - 1)
    def _():
        pl.semaphore_signal(
            barrier,
            inc=1,
            device_id={"seq": s, "mp": (z + 1) * 2 + y},
            device_id_type=pl.DeviceIdType.MESH,
        )

    pl.semaphore_signal(
        barrier,
        inc=1,
        device_id={"seq": s, "mp": z * 2 + yo},
        device_id_type=pl.DeviceIdType.MESH,
    )
    pl.semaphore_wait(barrier, slabs + jnp.where(z > 0, 1, 0) + jnp.where(z < nz - 1, 1, 0))

    lane = lax.broadcasted_iota(jnp.int32, (1, PAIR), 1)
    low_lane = lane < HD
    lane_masks = (
        jnp.where(low_lane, 1.0, 0.0).astype(BF16),
        jnp.where(low_lane, 0.0, 1.0).astype(BF16),
    )
    low_row = lax.broadcasted_iota(jnp.int32, (PAIR, 1), 0) < HD

    def pair_cols(p):
        return pl.ds(pl.multiple_of(p * PAIR, PAIR), PAIR)

    def chunk_cols(c):
        return pl.ds(pl.multiple_of(c * cols, cols), cols)

    def nth(k):
        up = nz - 1 - z
        low = jnp.where(k < up, nz - 1 - k, k - up)
        high = jnp.where(k < z, k, nz - 1 - (k - z))
        return jnp.where(k == nz - 1, z, jnp.where(z < nz // 2, low, high))

    def scatter_out(b, part, ysend, yrecv, ys, yr):
        def first(k, carry):
            t = nth(k)
            ysend[b, t] = part(b, t * 2 + yo)
            remote(ysend.at[b, t], yrecv.at[b, t], ys.at[b, t], yr.at[b, t], s, z * 2 + yo).start()
            return carry

        lax.fori_loop(0, nz, first, 0)

    def scatter_own(b, part):
        def own(k, carry):
            t = nth(k)
            own_part[b, t] = part(b, t * 2 + y)
            return carry

        lax.fori_loop(0, nz, own, 0)

    def scatter_in(b, yrecv, zsend, zrecv, yr, zs, zr):
        def join(t):
            arrived(yrecv.at[b, t], yr.at[b, t])
            tot[...] = own_part[b, t].astype(F32) + yrecv[b, t].astype(F32)

        def take(slot):
            arrived(zrecv.at[b, slot], zr.at[b, slot])
            tot[...] = tot[...] + zrecv[b, slot].astype(F32)

        def second(k, carry):
            t = nth(k)
            join(t)

            @pl.when((t > z) & (z > 0) | (t < z) & (z < nz - 1))
            def _():
                take(t)

            zsend[b, t] = tot[...].astype(BF16)

            @pl.when(t > z)
            def _():
                remote(
                    zsend.at[b, t], zrecv.at[b, t], zs.at[b, t], zr.at[b, t], s, (z + 1) * 2 + y
                ).start()

            @pl.when(t < z)
            def _():
                slot = jnp.where(t == z - 1, nz, t)
                remote(
                    zsend.at[b, t], zrecv.at[b, slot], zs.at[b, t], zr.at[b, slot], s, (z - 1) * 2 + y
                ).start()

            return carry

        lax.fori_loop(0, nz - 1, second, 0)
        join(z)

        @pl.when(z > 0)
        def _():
            take(z)

        @pl.when(z < nz - 1)
        def _():
            take(nz)

        return tot[...]

    def end_scatter(ysend, zsend, ys, zs):
        for b in range(BLOCKS):
            for k in range(nz):
                arrived(ysend.at[b, k], ys.at[b, k])

                @pl.when(z != k)
                def _():
                    arrived(zsend.at[b, k], zs.at[b, k])

    def final_scatter(part, base_ref, out_ref):
        for b in range(BLOCKS):
            scatter_out(b, part, ysend2, yrecv2, ys2_s, yr2_s)
        for b in range(BLOCKS):
            scatter_own(b, part)
        for b in range(BLOCKS):
            at = slice(b * sub, (b + 1) * sub)
            total = scatter_in(b, yrecv2, zsend2, zrecv2, yr2_s, zs2_s, zr2_s)
            out_ref[at, :] = (base_ref[at, :].astype(F32) + total).astype(BF16)

    def to_partner(c, t, b):
        remote(gath.at[c, b], gath.at[c, b], gy_s.at[t, b], gy_r.at[t, b], s, z * 2 + yo).start()

    def to_above(c, t, b):
        @pl.when(z < nz - 1)
        def _():
            remote(
                gath.at[c, b], gath.at[c, b], gu_s.at[t, b], gz_r.at[t, b], s, (z + 1) * 2 + y
            ).start()

    def to_below(c, t, b):
        @pl.when(z > 0)
        def _():
            remote(
                gath.at[c, b], gath.at[c, b], gd_s.at[t, b], gz_r.at[t, b], s, (z - 1) * 2 + y
            ).start()

    def gather_start(b):
        to_above(g, z, b)
        to_below(g, z, b)
        to_partner(g, z, b)

    def gather(use):
        use(g)

        def around(k, carry):
            @pl.when(z >= k)
            def _():
                t = z - k
                c = t * 2 + y
                for b in range(BLOCKS):
                    arrived(gath.at[c, b], gz_r.at[t, b])
                    to_above(c, t, b)
                    to_partner(c, t, b)

            @pl.when(z + k < nz)
            def _():
                t = z + k
                c = t * 2 + y
                for b in range(BLOCKS):
                    arrived(gath.at[c, b], gz_r.at[t, b])
                    to_below(c, t, b)
                    to_partner(c, t, b)

            @pl.when(z >= k)
            def _():
                use((z - k) * 2 + y)

            @pl.when(z + k < nz)
            def _():
                use((z + k) * 2 + y)

            return carry

        lax.fori_loop(1, nz, around, 0)

        def finish(k, carry):
            def land(t):
                c = t * 2 + yo
                for b in range(BLOCKS):
                    arrived(gath.at[c, b], gy_r.at[t, b])
                use(c)

            @pl.when(z >= k)
            def _():
                land(z - k)

            @pl.when((k > 0) & (z + k < nz))
            def _():
                land(z + k)

            return carry

        lax.fori_loop(0, nz, finish, 0)

    def end_gather():
        for b in range(BLOCKS):
            for t in range(nz):
                c = t * 2 + y
                arrived(gath.at[c, b], gy_s.at[t, b])

                @pl.when((z >= t) & (z < nz - 1))
                def _():
                    arrived(gath.at[c, b], gu_s.at[t, b])

                @pl.when((z <= t) & (z > 0))
                def _():
                    arrived(gath.at[c, b], gd_s.at[t, b])

    def whole_block(c):
        return gath[c].reshape(rows, cols)

    def joint_stats():
        top = stat_in[0, 0]
        for i in range(1, enc):
            top = jnp.maximum(top, stat_in[i, 0])
        total = jnp.zeros_like(top)
        dots = jnp.zeros_like(top)
        for i in range(enc):
            shift = jnp.exp(stat_in[i, 0] - top)
            total = total + shift * stat_in[i, 1]
            dots = dots + shift * stat_in[i, 2]
        return top, total, dots

    @pl.when(is_enc)
    def _():
        @pl.when(s + 1 < enc)
        def _():
            remote(
                kv_ref.at[:, pl.ds(rows - HALO, HALO)],
                kv_all.at[:, pl.ds(0, HALO)],
                halo_s.at[0],
                halo_r.at[0],
                s + 1,
                g,
            ).start()

        @pl.when(s > 0)
        def _():
            remote(
                kv_ref.at[:, pl.ds(0, HALO)],
                kv_all.at[:, pl.ds(HALO + rows, HALO)],
                halo_s.at[1],
                halo_r.at[1],
                s - 1,
                g,
            ).start()

        @pl.when(s == 0)
        def _():
            kv_all[:, pl.ds(0, HALO)] = jnp.zeros((2, HALO, cols), BF16)

        @pl.when(s == enc - 1)
        def _():
            kv_all[:, pl.ds(HALO + rows, HALO)] = jnp.zeros((2, HALO, cols), BF16)

        pltpu.make_async_copy(kv_ref, kv_all.at[:, pl.ds(HALO, rows)], kv_sem).wait()

        @pl.when(s > 0)
        def _():
            arrived(kv_all.at[:, pl.ds(0, HALO)], halo_r.at[0])

        @pl.when(s + 1 < enc)
        def _():
            arrived(kv_all.at[:, pl.ds(HALO + rows, HALO)], halo_r.at[1])

        span = sub + 2 * HALO

        def attn_part(b, c):
            return dot(ctx[b * sub : (b + 1) * sub, :], w_out[:, chunk_cols(c)]).astype(BF16)

        for b in range(BLOCKS):
            base = b * sub
            key_pos = s * rows + base - HALO + lax.broadcasted_iota(jnp.int32, (span, 1), 0)
            own_pos = s * rows + base + lax.broadcasted_iota(jnp.int32, (1, sub), 1)
            far = jnp.abs(key_pos - own_pos)
            own_at = pl.ds(pl.multiple_of(s * rows + base, sub), sub)
            in_doc = (key_pos >= bnd_ref[0:1, own_at]) & (key_pos <= bnd_ref[1:2, own_at])
            far_in = jnp.where(in_doc, far, jnp.int32(1 << 20))

            def local_pair(p, carry):
                at = pair_cols(p)
                q_pair = q_ref[base : base + sub, at]
                k_pair = kv_all[0, base : base + span, at]
                v_t = kv_all[1, base : base + span, at].T
                got = []
                for i in range(2):
                    sc = dot_nt(k_pair, q_pair * lane_masks[i]) * scale
                    sc = jnp.where(far_in <= win_ref[p * 2 + i], sc, LOW)
                    e = jnp.exp(sc - jnp.max(sc, axis=0, keepdims=True))
                    inv = 1.0 / jnp.sum(e, axis=0, keepdims=True)
                    got.append(dot(v_t, (e * inv).astype(BF16)))
                ctx[base : base + sub, at] = jnp.where(low_row, got[0], got[1]).T.astype(BF16)
                return carry

            lax.fori_loop(0, pairs, local_pair, 0)
            if b == 0:
                pltpu.make_async_copy(ow_ref.at[0], w_out, w_sem.at[0]).wait()
            scatter_out(b, attn_part, ysend, yrecv, ys_s, yr_s)
        for b in range(BLOCKS):
            scatter_own(b, attn_part)
        for b in range(BLOCKS):
            at = slice(b * sub, (b + 1) * sub)
            total = scatter_in(b, yrecv, zsend, zrecv, yr_s, zs_s, zr_s)
            hidden = (res_ref[at, :].astype(F32) + total).astype(BF16)
            gath[g, b] = hidden
            gather_start(b)
            states_ref[at, :] = hidden
        for i in range(2):
            acc[i] = jnp.zeros((rows, cols), F32)
        pltpu.make_async_copy(kw_ref, w_kv, w_sem.at[1]).wait()

        def project(c):
            block = whole_block(c)
            acc[0] = acc[0] + dot(block, w_kv[0, chunk_cols(c), :])
            acc[1] = acc[1] + dot(block, w_kv[1, chunk_cols(c), :])

        gather(project)
        kv_new[...] = acc[...].astype(BF16)
        arrived(dq, dq_r)
        arrived(dg, dg_r)

        tok_pos = s * rows + lax.broadcasted_iota(jnp.int32, (rows, 1), 0)
        seen = (tok_pos >= bnd_ref[0:1, enc * rows :]) & (tok_pos <= bnd_ref[1:2, enc * rows :])

        def cross_pair(p, carry):
            at = pair_cols(p)
            q_pair = dq[:, at]
            g_pair = dg[:, at]
            k_pair = kv_new[0, :, at]
            v_pair = kv_new[1, :, at]
            v_t = v_pair.T
            got = []
            for i in range(2):
                sc = dot_nt(k_pair, q_pair * lane_masks[i]) * scale
                sc = jnp.where(seen, sc, LOW)
                top = jnp.max(sc, axis=0, keepdims=True)
                e = jnp.exp(sc - top)
                dp = dot_nt(v_pair, g_pair * lane_masks[i])
                h = p * 2 + i
                e_buf[h] = e
                d_buf[h] = dp
                stat[0, pl.ds(h, 1), :] = top
                stat[1, pl.ds(h, 1), :] = jnp.sum(e, axis=0, keepdims=True)
                stat[2, pl.ds(h, 1), :] = jnp.sum(e * dp, axis=0, keepdims=True)
                got.append(dot(v_t, e.astype(BF16)))
            tbuf[pair_cols(p), :] = jnp.where(low_row, got[0], got[1]).astype(BF16)
            return carry

        lax.fori_loop(0, pairs, cross_pair, 0)
        for k in range(1, slabs):
            to = lax.rem(s + k, slabs)
            remote(stat, stat_in.at[s], st_s.at[k - 1], st_r.at[s], to, g).start()
        remote(tbuf, ctx_in.at[s], cx_s, cx_r.at[s], enc, g).start()
        stat_in[s] = stat[...]
        for k in range(1, enc):
            at = lax.rem(s + k, enc)
            arrived(stat_in.at[at], st_r.at[at])
        top, total, dots = joint_stats()
        fac[0] = jnp.exp(stat[0] - top) / total
        fac[1] = dots / total

        def grad_pair(p, carry):
            at = pair_cols(p)
            q_pair = dq[:, at]
            g_pair = dg[:, at]
            k_t = kv_new[0, :, at].T
            kg, vg, qg = [], [], []
            for i in range(2):
                h = p * 2 + i
                w = e_buf[h] * fac[0, pl.ds(h, 1), :]
                ds = (w * (d_buf[h] - fac[1, pl.ds(h, 1), :])).astype(BF16)
                vg.append(dot(w.astype(BF16), g_pair))
                kg.append(dot(ds, q_pair))
                qg.append(dot(k_t, ds))
            kvg[0, :, at] = (scale * jnp.where(low_lane, kg[0], kg[1])).astype(BF16)
            kvg[1, :, at] = jnp.where(low_lane, vg[0], vg[1]).astype(BF16)
            qg_buf[pair_cols(p), :] = (scale * jnp.where(low_row, qg[0], qg[1])).astype(BF16)
            return carry

        lax.fori_loop(0, pairs, grad_pair, 0)
        remote(qg_buf, qg_in.at[s], qg_s, qg_r.at[s], enc, g).start()
        def grad_part(b, c):
            at = slice(b * sub, (b + 1) * sub)
            return (
                dot_nt(kvg[0, at, :], w_kv[0, chunk_cols(c), :])
                + dot_nt(kvg[1, at, :], w_kv[1, chunk_cols(c), :])
            ).astype(BF16)

        final_scatter(grad_part, cot_ref, grads_ref)

        @pl.when(s + 1 < enc)
        def _():
            arrived(kv_ref.at[:, pl.ds(rows - HALO, HALO)], halo_s.at[0])

        @pl.when(s > 0)
        def _():
            arrived(kv_ref.at[:, pl.ds(0, HALO)], halo_s.at[1])

        end_scatter(ysend, zsend, ys_s, zs_s)
        end_gather()
        for k in range(1, slabs):
            arrived(stat, st_s.at[k - 1])
        arrived(tbuf, cx_s)
        arrived(qg_buf, qg_s)
        end_scatter(ysend2, zsend2, ys2_s, zs2_s)

    @pl.when(is_dec)
    def _():
        for k in range(enc):
            remote(q_ref, dq, dq_s.at[k], dq_r, k, g).start()
        for b in range(BLOCKS):
            gath[g, b] = cot_ref[b * sub : (b + 1) * sub, :]
            gather_start(b)
        acc[0] = jnp.zeros((rows, cols), F32)
        pltpu.make_async_copy(ow_ref.at[1], w_out, w_sem.at[0]).wait()

        def back(c):
            acc[0] = acc[0] + dot_nt(whole_block(c), w_out[:, chunk_cols(c)])

        gather(back)
        dg[...] = acc[0].astype(BF16)
        for k in range(enc):
            remote(dg, dg, dg_s.at[k], dg_r, k, g).start()
        for k in range(enc):
            arrived(stat_in.at[k], st_r.at[k])
        top, total, dots = joint_stats()
        shares = [jnp.exp(stat_in[k, 0] - top) / total for k in range(enc)]
        for k in range(enc):
            arrived(ctx_in.at[k], cx_r.at[k])
        for h in range(heads):
            at = slice(h * HD, (h + 1) * HD)
            part = jnp.zeros((HD, rows), F32)
            for k in range(enc):
                part = part + shares[k][h : h + 1, :] * ctx_in[k, at, :].astype(F32)
            d_buf[h, 0:HD, :] = part
        for p in range(pairs):
            both = jnp.concatenate([d_buf[2 * p, 0:HD, :], d_buf[2 * p + 1, 0:HD, :]], axis=0)
            ctx[:, p * PAIR : (p + 1) * PAIR] = both.T.astype(BF16)
        final_scatter(
            lambda b, c: dot(ctx[b * sub : (b + 1) * sub, :], w_out[:, chunk_cols(c)]).astype(BF16),
            res_ref,
            states_ref,
        )
        for k in range(enc):
            arrived(qg_in.at[k], qg_r.at[k])
        for p in range(pairs):
            at = slice(p * PAIR, (p + 1) * PAIR)
            part = jnp.zeros((PAIR, rows), F32)
            for k in range(enc):
                part = part + qg_in[k, at, :].astype(F32)
            grads_ref[:, at] = part.T.astype(BF16)
        for k in range(enc):
            arrived(q_ref, dq_s.at[k])
            arrived(dg, dg_s.at[k])
        end_gather()
        end_scatter(ysend2, zsend2, ys2_s, zs2_s)


def deliver(states_in, grads_in, states_out, grads_out):
    states_out[...] = states_in[...]
    grads_out[...] = grads_in[...]


def layer(slabs, groups, queries, keys_values, residual, cotangent, out_weight, kv_weight, bounds, windows):
    rows, cols = queries.shape
    heads = cols // HD
    nz = groups // 2
    enc = slabs - 1
    width = out_weight.shape[2]
    dma = pltpu.SemaphoreType.DMA
    blocks = lambda n: pltpu.VMEM((n, rows, cols), BF16)
    parts = lambda n: pltpu.VMEM((BLOCKS, n, rows // BLOCKS, cols), BF16)
    vmem = pl.BlockSpec(memory_space=pltpu.VMEM)
    hbm = pl.BlockSpec(memory_space=pl.ANY)
    states, grads = pl.pallas_call(
        functools.partial(layer_kernel, slabs, groups),
        out_shape=(jax.ShapeDtypeStruct((rows, cols), BF16),) * 2,
        in_specs=[vmem] * 4 + [hbm] * 2 + [vmem, pl.BlockSpec(memory_space=pltpu.SMEM)],
        out_specs=(vmem, vmem),
        scratch_shapes=[
            pltpu.VMEM((cols, width), BF16),
            pltpu.VMEM((2, width, cols), BF16),
            pltpu.VMEM((2, rows + 2 * HALO, cols), BF16),
            pltpu.VMEM((rows, cols), BF16),
            parts(nz),
            parts(nz),
            parts(nz),
            parts(nz),
            parts(nz + 1),
            parts(nz),
            parts(nz),
            parts(nz),
            parts(nz + 1),
            pltpu.VMEM((groups, BLOCKS, rows // BLOCKS, cols), BF16),
            pltpu.VMEM((2, rows, cols), F32),
            pltpu.VMEM((rows // BLOCKS, cols), F32),
            blocks(2),
            pltpu.VMEM((rows, cols), BF16),
            pltpu.VMEM((rows, cols), BF16),
            pltpu.VMEM((heads, rows, rows), F32),
            pltpu.VMEM((heads, rows, rows), F32),
            pltpu.VMEM((3, heads, rows), F32),
            pltpu.VMEM((slabs, 3, heads, rows), F32),
            pltpu.VMEM((2, heads, rows), F32),
            pltpu.VMEM((cols, rows), BF16),
            pltpu.VMEM((enc, cols, rows), BF16),
            pltpu.VMEM((cols, rows), BF16),
            pltpu.VMEM((enc, cols, rows), BF16),
            blocks(2),
            dma((2,)),
            dma,
            dma((2,)),
            dma((2,)),
        ]
        + [dma((BLOCKS, nz + 1))] * 8
        + [dma((nz, BLOCKS))] * 5
        + [
            dma((enc,)),
            dma,
            dma((enc,)),
            dma,
            dma((enc,)),
            dma((slabs,)),
            dma,
            dma((enc,)),
            dma,
            dma((enc,)),
        ],
        compiler_params=pltpu.CompilerParams(
            collective_id=0, has_side_effects=True, vmem_limit_bytes=60 * 1024 * 1024
        ),
    )(queries, keys_values, residual, cotangent, out_weight, kv_weight, bounds, windows)
    return pl.pallas_call(
        deliver,
        out_shape=(jax.ShapeDtypeStruct((rows, cols), BF16),) * 2,
        in_specs=[vmem] * 2,
        out_specs=(vmem, vmem),
    )(states, grads)


def one_decoder_slab(mesh):
    slabs, groups = mesh.shape["seq"], mesh.shape["mp"]
    return slabs - 3 * slabs // 4 == 1 and groups % 2 == 0


def solution(mesh):
    body = shards
    if one_decoder_slab(mesh):
        body = functools.partial(layer, mesh.shape["seq"], mesh.shape["mp"])

    return jax.shard_map(
        body,
        mesh=mesh,
        in_specs=(
            P("seq", "mp"),
            P(None, "seq", "mp"),
            P("seq", "mp"),
            P("seq", "mp"),
            P(None, "mp", None),
            P(None, None, "mp"),
            P(),
            P("mp"),
        ),
        out_specs=(P("seq", "mp"), P("seq", "mp")),
        check_vma=False,
    )
```

```python
import functools

import jax
import jax.numpy as jnp
from jax import lax
from jax.experimental import pallas as pl
from jax.experimental.pallas import tpu as pltpu
from jax.sharding import PartitionSpec as P

HD = 64
WIN = 127


def with_halo(cells, sides, width):
    for axis, dim in sides:
        count = lax.axis_size(axis)
        ends = count - 1
        head = lax.slice_in_dim(cells, 0, width, axis=dim)
        tail = lax.slice_in_dim(cells, cells.shape[dim] - width, cells.shape[dim], axis=dim)
        cells = jnp.concatenate(
            [
                lax.ppermute(tail, axis, [(i, (i + 1) % count) for i in range(ends)]),
                cells,
                lax.ppermute(head, axis, [((i + 1) % count, i) for i in range(ends)]),
            ],
            axis=dim,
        )
    return cells


def softmax_masked(scores, permitted):
    masked_scores = jnp.where(permitted, scores, -jnp.inf)
    row_top = jnp.max(masked_scores, axis=-1, keepdims=True)
    exp_scores = jnp.exp(masked_scores - row_top)
    return exp_scores / jnp.sum(exp_scores, axis=-1, keepdims=True)


def shards(queries, keys_values, residual, cotangent, out_weight, kv_weight, bounds, windows):
    row_count = queries.shape[0]
    col_count = queries.shape[1]
    head_count = col_count // HD
    slab_count = lax.axis_size("seq")
    enc_slabs = 3 * slab_count // 4
    dec_slabs = slab_count - enc_slabs
    enc_tokens = enc_slabs * row_count
    token_count = slab_count * row_count
    dec_tokens = token_count - enc_tokens
    slab_index = lax.axis_index("seq")
    is_enc = slab_index < enc_slabs
    score_scale = HD ** (-0.5)
    own_pos = slab_index * row_count + jnp.arange(row_count, dtype=jnp.int32)
    own_first = lax.dynamic_slice_in_dim(bounds[0], slab_index * row_count, row_count)
    own_last = lax.dynamic_slice_in_dim(bounds[1], slab_index * row_count, row_count)
    query_heads = queries.reshape(row_count, head_count, HD)
    slice_cols = residual.shape[1]
    res_full, cot_full = (
        lax.all_gather(residual, "mp", axis=1, tiled=True),
        lax.all_gather(cotangent, "mp", axis=1, tiled=True),
    )
    model_width = cot_full.shape[1]
    rim_keys = with_halo(keys_values, (("seq", 1),), WIN)

    def local_part():
        span_count = rim_keys.shape[1]
        key_pos = slab_index * row_count - WIN + jnp.arange(span_count, dtype=jnp.int32)
        key_heads = rim_keys[0].reshape(span_count, head_count, HD)
        value_heads = rim_keys[1].reshape(span_count, head_count, HD)
        scores = (
            jnp.einsum("qhd,khd->hqk", query_heads, key_heads, preferred_element_type=jnp.float32)
            * score_scale
        )
        in_document = (key_pos[None, :] >= own_first[:, None]) & (
            key_pos[None, :] <= own_last[:, None]
        )
        distance = jnp.abs(own_pos[:, None] - key_pos[None, :])
        permitted = in_document[None] & (distance[None] <= windows[:, None, None])
        rounded = softmax_masked(scores, permitted).astype(jnp.bfloat16)
        context = jnp.einsum(
            "hqk,khd->qhd", rounded, value_heads, preferred_element_type=jnp.float32
        ).astype(jnp.bfloat16)
        return jnp.dot(
            context.reshape(row_count, col_count), out_weight[0], preferred_element_type=jnp.float32
        )

    head_partial = lax.cond(
        is_enc, local_part, lambda: jnp.zeros((row_count, model_width), jnp.float32)
    )
    attn_sum = lax.psum(head_partial.astype(jnp.bfloat16), "mp").astype(jnp.float32)
    hidden_full = (res_full.astype(jnp.float32) + attn_sum).astype(jnp.bfloat16)
    encoder_out = lax.dynamic_slice_in_dim(
        hidden_full, lax.axis_index("mp") * slice_cols, slice_cols, 1
    )

    def project_keys():
        key_proj = jnp.dot(hidden_full, kv_weight[0], preferred_element_type=jnp.float32).astype(
            jnp.bfloat16
        )
        value_proj = jnp.dot(hidden_full, kv_weight[1], preferred_element_type=jnp.float32).astype(
            jnp.bfloat16
        )
        return jnp.stack([key_proj, value_proj])

    cross_kv = lax.cond(
        is_enc, project_keys, lambda: jnp.zeros((2, row_count, col_count), jnp.bfloat16)
    )

    def context_gradient():
        return lax.dot_general(
            cot_full, out_weight[1], (((1,), (1,)), ((), ())), preferred_element_type=jnp.float32
        ).astype(jnp.bfloat16)

    dec_queries = lax.all_gather(queries, "seq", axis=0, tiled=True)[enc_tokens:]
    dec_heads = dec_queries.reshape(dec_tokens, head_count, HD)
    dec_first = bounds[0, enc_tokens:]
    dec_last = bounds[1, enc_tokens:]
    in_document = (own_pos[None, :] >= dec_first[:, None]) & (own_pos[None, :] <= dec_last[:, None])
    key_heads = cross_kv[0].reshape(row_count, head_count, HD)
    value_heads = cross_kv[1].reshape(row_count, head_count, HD)
    scores = (
        jnp.einsum("qhd,khd->hqk", dec_heads, key_heads, preferred_element_type=jnp.float32)
        * score_scale
    )
    masked_scores = jnp.where(in_document[None], scores, -jnp.inf)
    row_top = lax.pmax(jnp.max(masked_scores, axis=2), "seq")
    exp_scores = jnp.exp(masked_scores - row_top[:, :, None])
    row_total = lax.psum(jnp.sum(exp_scores, axis=2), "seq")
    weights = exp_scores / row_total[:, :, None]
    rounded = weights.astype(jnp.bfloat16)
    partial_ctx = jnp.einsum(
        "hqk,khd->qhd", rounded, value_heads, preferred_element_type=jnp.float32
    ).reshape(dec_tokens, col_count)
    context_all = lax.psum(partial_ctx.astype(jnp.bfloat16), "seq")
    dec_offset = jnp.maximum(slab_index - enc_slabs, 0) * row_count
    context = lax.dynamic_slice_in_dim(context_all, dec_offset, row_count, 0)
    out_part = lax.cond(
        is_enc,
        lambda: jnp.zeros((row_count, model_width), jnp.float32),
        lambda: jnp.dot(context, out_weight[1], preferred_element_type=jnp.float32),
    )
    grad_own = lax.cond(
        is_enc, lambda: jnp.zeros((row_count, col_count), jnp.bfloat16), context_gradient
    )
    grad_all = lax.all_gather(grad_own, "seq", axis=0, tiled=True)[enc_tokens:]
    grad_heads = grad_all.reshape(dec_tokens, head_count, HD)
    row_dots = jnp.einsum(
        "qhd,qhd->hq",
        grad_heads,
        context_all.reshape(dec_tokens, head_count, HD),
        preferred_element_type=jnp.float32,
    )
    prob_grad = jnp.einsum(
        "qhd,khd->hqk", grad_heads, value_heads, preferred_element_type=jnp.float32
    )
    score_grad = (weights * (prob_grad - row_dots[:, :, None])).astype(jnp.bfloat16)
    grad_blocks = score_grad.reshape(head_count, dec_slabs, row_count, row_count)
    prob_blocks = rounded.reshape(head_count, dec_slabs, row_count, row_count)
    query_blocks = dec_heads.reshape(dec_slabs, row_count, head_count, HD)
    grad_rows = grad_heads.reshape(dec_slabs, row_count, head_count, HD)
    key_parts = (
        score_scale
        * jnp.einsum(
            "hsqk,sqhd->skhd", grad_blocks, query_blocks, preferred_element_type=jnp.float32
        )
    ).astype(jnp.bfloat16)
    value_parts = jnp.einsum(
        "hsqk,sqhd->skhd", prob_blocks, grad_rows, preferred_element_type=jnp.float32
    ).astype(jnp.bfloat16)
    key_grad = (
        jnp.sum(key_parts.astype(jnp.float32), axis=0)
        .astype(jnp.bfloat16)
        .reshape(row_count, col_count)
    )
    value_grad = (
        jnp.sum(value_parts.astype(jnp.float32), axis=0)
        .astype(jnp.bfloat16)
        .reshape(row_count, col_count)
    )
    query_terms = score_scale * jnp.einsum(
        "hqk,khd->qhd", score_grad, key_heads, preferred_element_type=jnp.float32
    )
    query_sum = lax.psum(
        query_terms.reshape(dec_tokens, col_count).astype(jnp.bfloat16), "seq"
    ).astype(jnp.float32)
    query_grad = lax.dynamic_slice_in_dim(query_sum, dec_offset, row_count, 0).astype(jnp.bfloat16)
    contract = (((1,), (1,)), ((), ()))
    grad_terms = lax.dot_general(
        key_grad, kv_weight[0], contract, preferred_element_type=jnp.float32
    ) + lax.dot_general(value_grad, kv_weight[1], contract, preferred_element_type=jnp.float32)
    final_term = jnp.where(is_enc, grad_terms, out_part)
    final_share = lax.psum_scatter(
        final_term.astype(jnp.bfloat16), "mp", scatter_dimension=1, tiled=True
    ).astype(jnp.float32)
    base_rows = jnp.where(is_enc, cotangent, residual).astype(jnp.float32)
    final_rows = (base_rows + final_share).astype(jnp.bfloat16)
    states_out = jnp.where(is_enc, encoder_out, final_rows)
    grad_states = jnp.where(is_enc, final_rows, query_grad)
    return (states_out, grad_states)


F32 = jnp.float32
BF16 = jnp.bfloat16
LOW = -1e30
PAIR = 2 * HD
HALO = 128
BLOCKS = 2
NT = (((1,), (1,)), ((), ()))


def dot(a, b):
    return jnp.dot(a, b, preferred_element_type=F32)


def dot_nt(a, b):
    return lax.dot_general(a, b, NT, preferred_element_type=F32)


def layer_kernel(
    slabs,
    groups,
    q_ref,
    kv_ref,
    res_ref,
    cot_ref,
    ow_ref,
    kw_ref,
    bnd_ref,
    win_ref,
    states_ref,
    grads_ref,
    w_out,
    w_kv,
    kv_all,
    ctx,
    own_part,
    ysend,
    yrecv,
    zsend,
    zrecv,
    ysend2,
    yrecv2,
    zsend2,
    zrecv2,
    gath,
    acc,
    tot,
    xrecv,
    xrecv2,
    kv_new,
    dq,
    dg,
    e_buf,
    d_buf,
    stat,
    stat_in,
    fac,
    tbuf,
    ctx_in,
    qg_buf,
    qg_in,
    kvg,
    w_sem,
    kv_sem,
    halo_s,
    halo_r,
    ys_s,
    yr_s,
    zs_s,
    zr_s,
    ys2_s,
    yr2_s,
    zs2_s,
    zr2_s,
    xr_s,
    xr2_s,
    gx_s,
    gx_r,
    gu_s,
    gd_s,
    gz_r,
    gy_s,
    gy_r,
    dq_s,
    dq_r,
    dg_s,
    dg_r,
    st_s,
    st_r,
    cx_s,
    cx_r,
    qg_s,
    qg_r,
):
    rows, cols = q_ref.shape
    pairs = cols // PAIR
    heads = cols // HD
    enc = slabs - 1
    sub = rows // BLOCKS
    nz = groups // 2
    scale = HD ** (-0.5)
    s = lax.axis_index("seq")
    g = lax.axis_index("mp")
    z = g // 2
    y = lax.rem(g, 2)
    yo = 1 - y
    near = z + 1 - 2 * lax.rem(z, 2)
    tail = BLOCKS - 1

    def remote(src, dst, send, recv, seq, mp):
        return pltpu.make_async_remote_copy(
            src_ref=src,
            dst_ref=dst,
            send_sem=send,
            recv_sem=recv,
            device_id={"seq": seq, "mp": mp},
            device_id_type=pl.DeviceIdType.MESH,
        )

    def arrived(dst, recv):
        pltpu.make_async_copy(dst, dst, recv).wait()

    is_enc = s < enc
    is_dec = s >= enc

    @pl.when(is_enc)
    def _():
        pltpu.make_async_copy(kv_ref, kv_all.at[:, pl.ds(HALO, rows)], kv_sem).start()
        pltpu.make_async_copy(ow_ref.at[0], w_out, w_sem.at[0]).start()
        pltpu.make_async_copy(kw_ref, w_kv, w_sem.at[1]).start()

    @pl.when(is_dec)
    def _():
        pltpu.make_async_copy(ow_ref.at[1], w_out, w_sem.at[0]).start()

    barrier = pltpu.get_barrier_semaphore()
    for k in range(1, slabs):
        pl.semaphore_signal(
            barrier,
            inc=1,
            device_id={"seq": lax.rem(s + k, slabs), "mp": g},
            device_id_type=pl.DeviceIdType.MESH,
        )

    @pl.when(z > 0)
    def _():
        pl.semaphore_signal(
            barrier,
            inc=1,
            device_id={"seq": s, "mp": (z - 1) * 2 + y},
            device_id_type=pl.DeviceIdType.MESH,
        )

    @pl.when(z < nz - 1)
    def _():
        pl.semaphore_signal(
            barrier,
            inc=1,
            device_id={"seq": s, "mp": (z + 1) * 2 + y},
            device_id_type=pl.DeviceIdType.MESH,
        )

    pl.semaphore_signal(
        barrier,
        inc=1,
        device_id={"seq": s, "mp": z * 2 + yo},
        device_id_type=pl.DeviceIdType.MESH,
    )
    pl.semaphore_wait(barrier, slabs + jnp.where(z > 0, 1, 0) + jnp.where(z < nz - 1, 1, 0))

    lane = lax.broadcasted_iota(jnp.int32, (1, PAIR), 1)
    low_lane = lane < HD
    lane_masks = (
        jnp.where(low_lane, 1.0, 0.0).astype(BF16),
        jnp.where(low_lane, 0.0, 1.0).astype(BF16),
    )
    low_row = lax.broadcasted_iota(jnp.int32, (PAIR, 1), 0) < HD

    def pair_cols(p):
        return pl.ds(pl.multiple_of(p * PAIR, PAIR), PAIR)

    def chunk_cols(c):
        return pl.ds(pl.multiple_of(c * cols, cols), cols)

    def nth(k):
        up = nz - 1 - z
        low = jnp.where(k < up, nz - 1 - k, k - up)
        high = jnp.where(k < z, k, nz - 1 - (k - z))
        return jnp.where(k == nz - 1, z, jnp.where(z < nz // 2, low, high))

    def scatter_out(b, part, ysend, yrecv, xrecv, ys, yr, xr):
        def first(k, carry):
            t = nth(k)
            ysend[b, t] = part(b, t * 2 + yo)
            over = remote(ysend.at[b, t], yrecv.at[b, t], ys.at[b, t], yr.at[b, t], s, z * 2 + yo)
            if b < tail:
                over.start()
            else:

                @pl.when((t != near) & (t != z))
                def _():
                    over.start()

                @pl.when(t == near)
                def _():
                    remote(ysend.at[b, t], xrecv, ys.at[b, t], xr, s, near * 2 + y).start()

            return carry

        lax.fori_loop(0, nz, first, 0)

    def scatter_own(b, part):
        def own(k, carry):
            t = nth(k)
            own_part[b, t] = part(b, t * 2 + y)
            return carry

        lax.fori_loop(0, nz, own, 0)

    def scatter_late(ysend, yrecv, xrecv, ys, yr, xr):
        arrived(xrecv, xr)
        ysend[tail, z] = (ysend[tail, z].astype(F32) + xrecv[...].astype(F32)).astype(BF16)
        remote(
            ysend.at[tail, z], yrecv.at[tail, z], ys.at[tail, z], yr.at[tail, z], s, z * 2 + yo
        ).start()

    def scatter_in(b, yrecv, zsend, zrecv, yr, zs, zr):
        def join(t):
            def both():
                arrived(yrecv.at[b, t], yr.at[b, t])
                tot[...] = own_part[b, t].astype(F32) + yrecv[b, t].astype(F32)

            if b < tail:
                both()
            else:

                @pl.when(t != near)
                def _():
                    both()

                @pl.when(t == near)
                def _():
                    tot[...] = own_part[b, t].astype(F32)

        def take(slot):
            arrived(zrecv.at[b, slot], zr.at[b, slot])
            tot[...] = tot[...] + zrecv[b, slot].astype(F32)

        def second(k, carry):
            t = nth(k)
            join(t)

            @pl.when((t > z) & (z > 0) | (t < z) & (z < nz - 1))
            def _():
                take(t)

            zsend[b, t] = tot[...].astype(BF16)

            @pl.when(t > z)
            def _():
                remote(
                    zsend.at[b, t], zrecv.at[b, t], zs.at[b, t], zr.at[b, t], s, (z + 1) * 2 + y
                ).start()

            @pl.when(t < z)
            def _():
                slot = jnp.where(t == z - 1, nz, t)
                remote(
                    zsend.at[b, t], zrecv.at[b, slot], zs.at[b, t], zr.at[b, slot], s, (z - 1) * 2 + y
                ).start()

            return carry

        lax.fori_loop(0, nz - 1, second, 0)
        join(z)

        @pl.when(z > 0)
        def _():
            take(z)

        @pl.when(z < nz - 1)
        def _():
            take(nz)

        return tot[...]

    def end_scatter(ysend, zsend, ys, zs):
        for b in range(BLOCKS):
            for k in range(nz):
                arrived(ysend.at[b, k], ys.at[b, k])

                @pl.when(z != k)
                def _():
                    arrived(zsend.at[b, k], zs.at[b, k])

    def final_scatter(part, base_ref, out_ref):
        for b in range(BLOCKS):
            scatter_out(b, part, ysend2, yrecv2, xrecv2, ys2_s, yr2_s, xr2_s)
        for b in range(BLOCKS):
            scatter_own(b, part)
        scatter_late(ysend2, yrecv2, xrecv2, ys2_s, yr2_s, xr2_s)
        for b in range(BLOCKS):
            at = slice(b * sub, (b + 1) * sub)
            total = scatter_in(b, yrecv2, zsend2, zrecv2, yr2_s, zs2_s, zr2_s)
            out_ref[at, :] = (base_ref[at, :].astype(F32) + total).astype(BF16)

    def to_partner(c, t, b):
        remote(gath.at[c, b], gath.at[c, b], gy_s.at[t, b], gy_r.at[t, b], s, z * 2 + yo).start()

    def to_above(c, t, b):
        @pl.when(z < nz - 1)
        def _():
            remote(
                gath.at[c, b], gath.at[c, b], gu_s.at[t, b], gz_r.at[t, b], s, (z + 1) * 2 + y
            ).start()

    def to_below(c, t, b):
        @pl.when(z > 0)
        def _():
            remote(
                gath.at[c, b], gath.at[c, b], gd_s.at[t, b], gz_r.at[t, b], s, (z - 1) * 2 + y
            ).start()

    def gather_start(b):
        to_above(g, z, b)
        to_below(g, z, b)
        to_partner(g, z, b)

    def gather(use):
        use(g)
        mate = z * 2 + yo
        for b in range(BLOCKS):
            arrived(gath.at[mate, b], gy_r.at[z, b])
        remote(gath.at[mate, tail], gath.at[mate, tail], gx_s, gx_r, s, near * 2 + y).start()

        def forward(c, t, b):
            if b < tail:
                to_partner(c, t, b)
            else:

                @pl.when(t != near)
                def _():
                    to_partner(c, t, b)

        def around(k, carry):
            @pl.when(z >= k)
            def _():
                t = z - k
                c = t * 2 + y
                for b in range(BLOCKS):
                    arrived(gath.at[c, b], gz_r.at[t, b])
                    to_above(c, t, b)
                    forward(c, t, b)

            @pl.when(z + k < nz)
            def _():
                t = z + k
                c = t * 2 + y
                for b in range(BLOCKS):
                    arrived(gath.at[c, b], gz_r.at[t, b])
                    to_below(c, t, b)
                    forward(c, t, b)

            @pl.when(z >= k)
            def _():
                use((z - k) * 2 + y)

            @pl.when(z + k < nz)
            def _():
                use((z + k) * 2 + y)

            return carry

        lax.fori_loop(1, nz, around, 0)

        def finish(k, carry):
            def land(t):
                c = t * 2 + yo
                for b in range(BLOCKS):
                    if b < tail:

                        @pl.when(t != z)
                        def _():
                            arrived(gath.at[c, b], gy_r.at[t, b])

                    else:

                        @pl.when((t != z) & (t != near))
                        def _():
                            arrived(gath.at[c, b], gy_r.at[t, b])

                        @pl.when(t == near)
                        def _():
                            arrived(gath.at[c, b], gx_r)

                use(c)

            @pl.when(z >= k)
            def _():
                land(z - k)

            @pl.when((k > 0) & (z + k < nz))
            def _():
                land(z + k)

            return carry

        lax.fori_loop(0, nz, finish, 0)

    def end_gather():
        arrived(gath.at[g, tail], gx_s)
        for b in range(BLOCKS):
            for t in range(nz):
                c = t * 2 + y
                if b < tail:
                    arrived(gath.at[c, b], gy_s.at[t, b])
                else:

                    @pl.when(near != t)
                    def _():
                        arrived(gath.at[c, b], gy_s.at[t, b])

                @pl.when((z >= t) & (z < nz - 1))
                def _():
                    arrived(gath.at[c, b], gu_s.at[t, b])

                @pl.when((z <= t) & (z > 0))
                def _():
                    arrived(gath.at[c, b], gd_s.at[t, b])

    def whole_block(c):
        return gath[c].reshape(rows, cols)

    def joint_stats():
        top = stat_in[0, 0]
        for i in range(1, enc):
            top = jnp.maximum(top, stat_in[i, 0])
        total = jnp.zeros_like(top)
        dots = jnp.zeros_like(top)
        for i in range(enc):
            shift = jnp.exp(stat_in[i, 0] - top)
            total = total + shift * stat_in[i, 1]
            dots = dots + shift * stat_in[i, 2]
        return top, total, dots

    @pl.when(is_enc)
    def _():
        @pl.when(s + 1 < enc)
        def _():
            remote(
                kv_ref.at[:, pl.ds(rows - HALO, HALO)],
                kv_all.at[:, pl.ds(0, HALO)],
                halo_s.at[0],
                halo_r.at[0],
                s + 1,
                g,
            ).start()

        @pl.when(s > 0)
        def _():
            remote(
                kv_ref.at[:, pl.ds(0, HALO)],
                kv_all.at[:, pl.ds(HALO + rows, HALO)],
                halo_s.at[1],
                halo_r.at[1],
                s - 1,
                g,
            ).start()

        @pl.when(s == 0)
        def _():
            kv_all[:, pl.ds(0, HALO)] = jnp.zeros((2, HALO, cols), BF16)

        @pl.when(s == enc - 1)
        def _():
            kv_all[:, pl.ds(HALO + rows, HALO)] = jnp.zeros((2, HALO, cols), BF16)

        pltpu.make_async_copy(kv_ref, kv_all.at[:, pl.ds(HALO, rows)], kv_sem).wait()

        @pl.when(s > 0)
        def _():
            arrived(kv_all.at[:, pl.ds(0, HALO)], halo_r.at[0])

        @pl.when(s + 1 < enc)
        def _():
            arrived(kv_all.at[:, pl.ds(HALO + rows, HALO)], halo_r.at[1])

        span = sub + 2 * HALO

        def attn_part(b, c):
            return dot(ctx[b * sub : (b + 1) * sub, :], w_out[:, chunk_cols(c)]).astype(BF16)

        for b in range(BLOCKS):
            base = b * sub
            key_pos = s * rows + base - HALO + lax.broadcasted_iota(jnp.int32, (span, 1), 0)
            own_pos = s * rows + base + lax.broadcasted_iota(jnp.int32, (1, sub), 1)
            far = jnp.abs(key_pos - own_pos)
            own_at = pl.ds(pl.multiple_of(s * rows + base, sub), sub)
            in_doc = (key_pos >= bnd_ref[0:1, own_at]) & (key_pos <= bnd_ref[1:2, own_at])
            far_in = jnp.where(in_doc, far, jnp.int32(1 << 20))

            def local_pair(p, carry):
                at = pair_cols(p)
                q_pair = q_ref[base : base + sub, at]
                k_pair = kv_all[0, base : base + span, at]
                v_t = kv_all[1, base : base + span, at].T
                got = []
                for i in range(2):
                    sc = dot_nt(k_pair, q_pair * lane_masks[i]) * scale
                    sc = jnp.where(far_in <= win_ref[p * 2 + i], sc, LOW)
                    e = jnp.exp(sc - jnp.max(sc, axis=0, keepdims=True))
                    inv = 1.0 / jnp.sum(e, axis=0, keepdims=True)
                    got.append(dot(v_t, (e * inv).astype(BF16)))
                ctx[base : base + sub, at] = jnp.where(low_row, got[0], got[1]).T.astype(BF16)
                return carry

            lax.fori_loop(0, pairs, local_pair, 0)
            if b == 0:
                pltpu.make_async_copy(ow_ref.at[0], w_out, w_sem.at[0]).wait()
            scatter_out(b, attn_part, ysend, yrecv, xrecv, ys_s, yr_s, xr_s)
        for b in range(BLOCKS):
            scatter_own(b, attn_part)
        scatter_late(ysend, yrecv, xrecv, ys_s, yr_s, xr_s)
        for b in range(BLOCKS):
            at = slice(b * sub, (b + 1) * sub)
            total = scatter_in(b, yrecv, zsend, zrecv, yr_s, zs_s, zr_s)
            hidden = (res_ref[at, :].astype(F32) + total).astype(BF16)
            gath[g, b] = hidden
            gather_start(b)
            states_ref[at, :] = hidden
        for i in range(2):
            acc[i] = jnp.zeros((rows, cols), F32)
        pltpu.make_async_copy(kw_ref, w_kv, w_sem.at[1]).wait()

        def project(c):
            block = whole_block(c)
            acc[0] = acc[0] + dot(block, w_kv[0, chunk_cols(c), :])
            acc[1] = acc[1] + dot(block, w_kv[1, chunk_cols(c), :])

        gather(project)
        kv_new[...] = acc[...].astype(BF16)
        arrived(dq, dq_r)
        arrived(dg, dg_r)

        tok_pos = s * rows + lax.broadcasted_iota(jnp.int32, (rows, 1), 0)
        seen = (tok_pos >= bnd_ref[0:1, enc * rows :]) & (tok_pos <= bnd_ref[1:2, enc * rows :])

        def cross_pair(p, carry):
            at = pair_cols(p)
            q_pair = dq[:, at]
            g_pair = dg[:, at]
            k_pair = kv_new[0, :, at]
            v_pair = kv_new[1, :, at]
            v_t = v_pair.T
            got = []
            for i in range(2):
                sc = dot_nt(k_pair, q_pair * lane_masks[i]) * scale
                sc = jnp.where(seen, sc, LOW)
                top = jnp.max(sc, axis=0, keepdims=True)
                e = jnp.exp(sc - top)
                dp = dot_nt(v_pair, g_pair * lane_masks[i])
                h = p * 2 + i
                e_buf[h] = e
                d_buf[h] = dp
                stat[0, pl.ds(h, 1), :] = top
                stat[1, pl.ds(h, 1), :] = jnp.sum(e, axis=0, keepdims=True)
                stat[2, pl.ds(h, 1), :] = jnp.sum(e * dp, axis=0, keepdims=True)
                got.append(dot(v_t, e.astype(BF16)))
            tbuf[pair_cols(p), :] = jnp.where(low_row, got[0], got[1]).astype(BF16)
            return carry

        lax.fori_loop(0, pairs, cross_pair, 0)
        for k in range(1, slabs):
            to = lax.rem(s + k, slabs)
            remote(stat, stat_in.at[s], st_s.at[k - 1], st_r.at[s], to, g).start()
        remote(tbuf, ctx_in.at[s], cx_s, cx_r.at[s], enc, g).start()
        stat_in[s] = stat[...]
        for k in range(1, enc):
            at = lax.rem(s + k, enc)
            arrived(stat_in.at[at], st_r.at[at])
        top, total, dots = joint_stats()
        fac[0] = jnp.exp(stat[0] - top) / total
        fac[1] = dots / total

        def grad_pair(p, carry):
            at = pair_cols(p)
            q_pair = dq[:, at]
            g_pair = dg[:, at]
            k_t = kv_new[0, :, at].T
            kg, vg, qg = [], [], []
            for i in range(2):
                h = p * 2 + i
                w = e_buf[h] * fac[0, pl.ds(h, 1), :]
                ds = (w * (d_buf[h] - fac[1, pl.ds(h, 1), :])).astype(BF16)
                vg.append(dot(w.astype(BF16), g_pair))
                kg.append(dot(ds, q_pair))
                qg.append(dot(k_t, ds))
            kvg[0, :, at] = (scale * jnp.where(low_lane, kg[0], kg[1])).astype(BF16)
            kvg[1, :, at] = jnp.where(low_lane, vg[0], vg[1]).astype(BF16)
            qg_buf[pair_cols(p), :] = (scale * jnp.where(low_row, qg[0], qg[1])).astype(BF16)
            return carry

        lax.fori_loop(0, pairs, grad_pair, 0)
        remote(qg_buf, qg_in.at[s], qg_s, qg_r.at[s], enc, g).start()
        def grad_part(b, c):
            at = slice(b * sub, (b + 1) * sub)
            return (
                dot_nt(kvg[0, at, :], w_kv[0, chunk_cols(c), :])
                + dot_nt(kvg[1, at, :], w_kv[1, chunk_cols(c), :])
            ).astype(BF16)

        final_scatter(grad_part, cot_ref, grads_ref)

        @pl.when(s + 1 < enc)
        def _():
            arrived(kv_ref.at[:, pl.ds(rows - HALO, HALO)], halo_s.at[0])

        @pl.when(s > 0)
        def _():
            arrived(kv_ref.at[:, pl.ds(0, HALO)], halo_s.at[1])

        end_scatter(ysend, zsend, ys_s, zs_s)
        end_gather()
        for k in range(1, slabs):
            arrived(stat, st_s.at[k - 1])
        arrived(tbuf, cx_s)
        arrived(qg_buf, qg_s)
        end_scatter(ysend2, zsend2, ys2_s, zs2_s)

    @pl.when(is_dec)
    def _():
        for k in range(enc):
            remote(q_ref, dq, dq_s.at[k], dq_r, k, g).start()
        for b in range(BLOCKS):
            gath[g, b] = cot_ref[b * sub : (b + 1) * sub, :]
            gather_start(b)
        acc[0] = jnp.zeros((rows, cols), F32)
        pltpu.make_async_copy(ow_ref.at[1], w_out, w_sem.at[0]).wait()

        def back(c):
            acc[0] = acc[0] + dot_nt(whole_block(c), w_out[:, chunk_cols(c)])

        gather(back)
        dg[...] = acc[0].astype(BF16)
        for k in range(enc):
            remote(dg, dg, dg_s.at[k], dg_r, k, g).start()
        for k in range(enc):
            arrived(stat_in.at[k], st_r.at[k])
        top, total, dots = joint_stats()
        shares = [jnp.exp(stat_in[k, 0] - top) / total for k in range(enc)]
        for k in range(enc):
            arrived(ctx_in.at[k], cx_r.at[k])
        for h in range(heads):
            at = slice(h * HD, (h + 1) * HD)
            part = jnp.zeros((HD, rows), F32)
            for k in range(enc):
                part = part + shares[k][h : h + 1, :] * ctx_in[k, at, :].astype(F32)
            d_buf[h, 0:HD, :] = part
        for p in range(pairs):
            both = jnp.concatenate([d_buf[2 * p, 0:HD, :], d_buf[2 * p + 1, 0:HD, :]], axis=0)
            ctx[:, p * PAIR : (p + 1) * PAIR] = both.T.astype(BF16)
        final_scatter(
            lambda b, c: dot(ctx[b * sub : (b + 1) * sub, :], w_out[:, chunk_cols(c)]).astype(BF16),
            res_ref,
            states_ref,
        )
        for k in range(enc):
            arrived(qg_in.at[k], qg_r.at[k])
        for p in range(pairs):
            at = slice(p * PAIR, (p + 1) * PAIR)
            part = jnp.zeros((PAIR, rows), F32)
            for k in range(enc):
                part = part + qg_in[k, at, :].astype(F32)
            grads_ref[:, at] = part.T.astype(BF16)
        for k in range(enc):
            arrived(q_ref, dq_s.at[k])
            arrived(dg, dg_s.at[k])
        end_gather()
        end_scatter(ysend2, zsend2, ys2_s, zs2_s)


def deliver(states_in, grads_in, states_out, grads_out):
    states_out[...] = states_in[...]
    grads_out[...] = grads_in[...]


def layer(slabs, groups, queries, keys_values, residual, cotangent, out_weight, kv_weight, bounds, windows):
    rows, cols = queries.shape
    heads = cols // HD
    nz = groups // 2
    enc = slabs - 1
    width = out_weight.shape[2]
    dma = pltpu.SemaphoreType.DMA
    blocks = lambda n: pltpu.VMEM((n, rows, cols), BF16)
    parts = lambda n: pltpu.VMEM((BLOCKS, n, rows // BLOCKS, cols), BF16)
    vmem = pl.BlockSpec(memory_space=pltpu.VMEM)
    hbm = pl.BlockSpec(memory_space=pl.ANY)
    states, grads = pl.pallas_call(
        functools.partial(layer_kernel, slabs, groups),
        out_shape=(jax.ShapeDtypeStruct((rows, cols), BF16),) * 2,
        in_specs=[vmem] * 4 + [hbm] * 2 + [vmem, pl.BlockSpec(memory_space=pltpu.SMEM)],
        out_specs=(vmem, vmem),
        scratch_shapes=[
            pltpu.VMEM((cols, width), BF16),
            pltpu.VMEM((2, width, cols), BF16),
            pltpu.VMEM((2, rows + 2 * HALO, cols), BF16),
            pltpu.VMEM((rows, cols), BF16),
            parts(nz),
            parts(nz),
            parts(nz),
            parts(nz),
            parts(nz + 1),
            parts(nz),
            parts(nz),
            parts(nz),
            parts(nz + 1),
            pltpu.VMEM((groups, BLOCKS, rows // BLOCKS, cols), BF16),
            pltpu.VMEM((2, rows, cols), F32),
            pltpu.VMEM((rows // BLOCKS, cols), F32),
            pltpu.VMEM((rows // BLOCKS, cols), BF16),
            pltpu.VMEM((rows // BLOCKS, cols), BF16),
            blocks(2),
            pltpu.VMEM((rows, cols), BF16),
            pltpu.VMEM((rows, cols), BF16),
            pltpu.VMEM((heads, rows, rows), F32),
            pltpu.VMEM((heads, rows, rows), F32),
            pltpu.VMEM((3, heads, rows), F32),
            pltpu.VMEM((slabs, 3, heads, rows), F32),
            pltpu.VMEM((2, heads, rows), F32),
            pltpu.VMEM((cols, rows), BF16),
            pltpu.VMEM((enc, cols, rows), BF16),
            pltpu.VMEM((cols, rows), BF16),
            pltpu.VMEM((enc, cols, rows), BF16),
            blocks(2),
            dma((2,)),
            dma,
            dma((2,)),
            dma((2,)),
        ]
        + [dma((BLOCKS, nz + 1))] * 8
        + [dma] * 4
        + [dma((nz, BLOCKS))] * 5
        + [
            dma((enc,)),
            dma,
            dma((enc,)),
            dma,
            dma((enc,)),
            dma((slabs,)),
            dma,
            dma((enc,)),
            dma,
            dma((enc,)),
        ],
        compiler_params=pltpu.CompilerParams(
            collective_id=0, has_side_effects=True, vmem_limit_bytes=60 * 1024 * 1024
        ),
    )(queries, keys_values, residual, cotangent, out_weight, kv_weight, bounds, windows)
    return pl.pallas_call(
        deliver,
        out_shape=(jax.ShapeDtypeStruct((rows, cols), BF16),) * 2,
        in_specs=[vmem] * 2,
        out_specs=(vmem, vmem),
    )(states, grads)


def one_decoder_slab(mesh):
    slabs, groups = mesh.shape["seq"], mesh.shape["mp"]
    return slabs - 3 * slabs // 4 == 1 and groups % 4 == 0


def solution(mesh):
    body = shards
    if one_decoder_slab(mesh):
        body = functools.partial(layer, mesh.shape["seq"], mesh.shape["mp"])

    return jax.shard_map(
        body,
        mesh=mesh,
        in_specs=(
            P("seq", "mp"),
            P(None, "seq", "mp"),
            P("seq", "mp"),
            P("seq", "mp"),
            P(None, "mp", None),
            P(None, None, "mp"),
            P(),
            P("mp"),
        ),
        out_specs=(P("seq", "mp"), P("seq", "mp")),
        check_vma=False,
    )
```
